128 devices in a mesh: space: 16 (over z, x_lo, core), samp: 8 (over y, x_hi).
Axes of the slice: x: 4 (x_hi: 2, x_lo: 2; x = x_hi * 2 + x_lo), y: 4, z: 4, core: 2. Of those that a mesh axis runs over, the one named last changes fastest.
Arguments:
- basis_u: bfloat16 [128, 32, 8, 128], P('samp', 'space'), may hold values from -0.75 to 0.75
- basis_v: bfloat16 [128, 65536], P('space', 'samp'), may hold values from -0.75 to 0.75
- core_s: float32 [128, 128], replicated, may hold values from -4 to 4
- face_class: int32 [6, 32, 8, 128], P(None, 'space'), may hold values from 0 to 3
- sample_class: int32 [65536], P('samp'), may hold values from 0 to 3
Outputs:
- k_new: float32 [128, 32, 8, 128], P('samp', 'space')
- l_new: float32 [128, 65536], P('space', 'samp')
The draws below stay inside these ranges and needn't reach their ends.
All inputs are finite; a program needn't handle non-finite values.
Results may differ from the reference program's by a relative error of at most 0.0046.
Values may be sent and summed in bfloat16 or wider, within the bound.
No kernel may reach another device: no remote copies, remote signals or barrier semaphores. Data moves between devices by JAX's collectives and lax.ppermute only.
A program may use at most 64 MiB of HBM per device.

```python
import jax
import jax.numpy as jnp
from jax import lax

NY = 8
NZ = 128
R = 128
NX = 32
CELLS = 32768
NSAMP = 65536


def place_ends(drawn, stream_key, smallest, largest):
    extent = drawn.shape
    spot = [jax.random.randint(jax.random.fold_in(stream_key, axis), (), 0, extent[axis]) for axis in range(len(extent))]
    drawn = drawn.at[tuple(spot)].set(smallest)
    longest = extent.index(max(extent))
    spot[longest] = (spot[longest] + 1) % extent[longest]
    return drawn.at[tuple(spot)].set(largest)


def raised(entries, rng, source, target, parts, factor):
    owner, partner = [(jnp.arange(entries.shape[position]) // (entries.shape[position] // parts)).reshape([-1 if axis == position else 1 for axis in range(entries.ndim)]) for position in (source, target)]
    chosen = jax.random.permutation(rng, parts)[partner]
    strong = (owner == chosen) | (owner == (partner + parts // 2) % parts)
    return jnp.where(strong, factor * entries, entries)


def level_of(own_key, shape, pieces, low, top_value):
    loudness, own = 1.0, jax.random.fold_in(own_key, 6)
    for position, shards_of in pieces:
        steps = jnp.exp(jax.random.uniform(jax.random.fold_in(own, position), (shards_of,), jnp.float32, low / len(pieces), top_value / len(pieces)))
        loudness = loudness * jnp.repeat(steps, shape[position] // shards_of).reshape([-1 if axis == position else 1 for axis in range(len(shape))])
    return loudness


def centred(stream_key, shape, scale, most, cuts=(), kind=jnp.bfloat16):
    gain = level_of(stream_key, shape, cuts, -0.22, 0.18) if cuts else 1.0
    result = jax.random.normal(stream_key, shape, jnp.float32) * scale * gain
    return jnp.minimum(jnp.maximum(result, -most), most).astype(kind)


def heavy_noise(own_key, extent, scale, bound, cuts, heavy, held_as=jnp.bfloat16):
    values = scale * jax.random.normal(own_key, extent, jnp.float32)
    if cuts:
        values = values * level_of(own_key, extent, cuts, -0.22, 0.18)
    return jnp.clip(raised(values, jax.random.fold_in(own_key, 3), *heavy), -bound, bound).astype(held_as)


def setup_inputs(seed: int = 0) -> dict:
    splits = jax.random.split(jax.random.key(seed), 6)
    basis_u = heavy_noise(splits[0], (R, NX, NY, NZ), R ** -0.5, 0.75, ((0, 8), (1, 16)), (1, 0, 16, 2.0))
    basis_v = heavy_noise(splits[1], (R, NSAMP), R ** -0.5, 0.75, ((0, 16), (1, 8)), (1, 0, 16, 2.0))
    core_s = centred(splits[2], (R, R), 1.0, 4.0, (), jnp.float32)
    face_class = place_ends(jax.random.randint(splits[3], (6, NX, NY, NZ), 0, 4), jax.random.fold_in(splits[3], 1), 0, 3).astype(jnp.int32)
    sample_class = place_ends(jax.random.randint(splits[4], (NSAMP,), 0, 4), jax.random.fold_in(splits[4], 1), 0, 3).astype(jnp.int32)
    return {"basis_u": basis_u, "basis_v": basis_v, "core_s": core_s, "face_class": face_class, "sample_class": sample_class}


step_size = 0.1


def laplace_of(k_old, face_class):
    weight = 0.25 * jnp.exp2(face_class.astype(jnp.float32))[..., None]
    padded_grid = jnp.pad(k_old.astype(jnp.float32), ((1, 1), (1, 1), (1, 1), (0, 0)))
    centre = padded_grid[1:-1, 1:-1, 1:-1]
    beside_all = (padded_grid[:-2, 1:-1, 1:-1], padded_grid[2:, 1:-1, 1:-1],
              padded_grid[1:-1, :-2, 1:-1], padded_grid[1:-1, 2:, 1:-1],
              padded_grid[1:-1, 1:-1, :-2], padded_grid[1:-1, 1:-1, 2:])
    summed = jnp.zeros_like(centre)
    for side_index in range(6):
        summed = summed + weight[side_index] * (beside_all[side_index] - centre)
    return summed


def reference(basis_u, basis_v, core_s, face_class, sample_class):
    core_b = core_s.astype(jnp.bfloat16)
    u_rows = basis_u.reshape(R, -1).T
    v_rows = basis_v.T
    k_flat = jnp.dot(u_rows, core_b, preferred_element_type=jnp.float32).astype(jnp.bfloat16)
    k_old = k_flat.reshape(NX, NY, NZ, R)
    laplace = laplace_of(k_old, face_class)
    lap_b = laplace.reshape(-1, R).astype(jnp.bfloat16)
    growth = 0.5 + 0.5 * sample_class.astype(jnp.float32)
    block_rows = min(512, NSAMP)
    block_count = NSAMP // block_rows
    v_blocks = v_rows.reshape(block_count, block_rows, R)
    g_blocks = growth.reshape(block_count, block_rows)

    def tile_step(accumulated, block_pair):
        v_block, g_block = block_pair
        sample_field = lax.dot_general(k_flat, v_block, (((1,), (1,)), ((), ())), preferred_element_type=jnp.float32)
        reaction = (g_block[None, :] * sample_field - sample_field * sample_field * sample_field).astype(jnp.bfloat16)
        accumulated = accumulated + jnp.dot(reaction, v_block, preferred_element_type=jnp.float32)
        onto_u = lax.dot_general(reaction, u_rows, (((0,), (0,)), ((), ())), preferred_element_type=jnp.float32)
        return accumulated, onto_u

    start_acc = jnp.zeros((CELLS, R), jnp.float32)
    accumulated, onto_blocks = lax.scan(tile_step, start_acc, (v_blocks, g_blocks))
    k_proj = accumulated * (R / NSAMP)
    k_cells = k_old.astype(jnp.float32) + step_size * (laplace + k_proj.reshape(NX, NY, NZ, R))
    moment = lax.dot_general(u_rows, lap_b, (((0,), (0,)), ((), ())), preferred_element_type=jnp.float32) * (R / CELLS)
    l_old = lax.dot_general(v_rows, core_b, (((1,), (1,)), ((), ())), preferred_element_type=jnp.float32)
    l_proj = onto_blocks.reshape(NSAMP, R) * (R / CELLS)
    side_term = jnp.dot(v_rows.astype(jnp.float32), moment.T, precision=lax.Precision.HIGHEST)
    l_rows = l_old + step_size * (side_term + l_proj)
    return jnp.transpose(k_cells, (3, 0, 1, 2)), l_rows.T
```

```python
import functools

import jax
import jax.numpy as jnp
from jax import lax
from jax.experimental import pallas as pl
from jax.experimental.pallas import tpu as pltpu
from jax.sharding import Mesh, PartitionSpec as P

step_size = 0.1
SPACE = ("z", "xl", "c")
SAMP = ("y", "xh")
CHUNKS = 2
bf16, f32 = jnp.bfloat16, jnp.float32


def dot(a, b, ca, cb):
    return lax.dot_general(a, b, (((ca,), (cb,)), ((), ())), preferred_element_type=f32)


def whole(shape):
    return pl.BlockSpec(shape, lambda *_: (0,) * len(shape))


def call(body, outs, grid=None, in_specs=None, out_specs=None, **kw):
    extra = {}
    if grid is not None:
        extra = dict(grid=grid, in_specs=in_specs, out_specs=out_specs)
    return pl.pallas_call(
        body,
        out_shape=[jax.ShapeDtypeStruct(s, d) for s, d in outs],
        compiler_params=pltpu.CompilerParams(vmem_limit_bytes=56 << 20),
        **extra,
        **kw,
    )


def prep_body(c_ref, own_ref, oth_ref, core_ref, k_ref, ko_ref, kt_ref, halo_ref):
    core_b = core_ref[...].astype(bf16)
    cells = own_ref.shape[1]
    half = cells // 2
    k_own = dot(core_b, own_ref[...], 0, 0).astype(bf16)
    k_oth = dot(core_b, oth_ref[...], 0, 0).astype(bf16)
    k_ref[...] = k_own
    kt_ref[:cells, :] = k_own.T
    kt_ref[cells:, :] = k_oth.T
    first = c_ref[0] == 0

    @pl.when(first)
    def _():
        halo_ref[...] = k_own[:, :half]
        ko_ref[...] = k_oth[:, :half]

    @pl.when(jnp.logical_not(first))
    def _():
        halo_ref[...] = k_own[:, half:]
        ko_ref[...] = k_oth[:, half:]


def lap_body(rows, cols, c_ref, k_ref, near_ref, halo_ref, face_ref, u_ref, base_ref, m_ref, base_s, lap_s):
    first = c_ref[0] == 0
    near = near_ref[...].astype(f32)
    halo = halo_ref[...].astype(f32)
    before = jnp.where(first, halo, near)
    after = jnp.where(first, near, halo)
    plane = rows * cols
    lane = lax.broadcasted_iota(jnp.int32, (1, cols), 1)
    for x in range(2):
        for y in range(rows):
            at = (x * rows + y) * cols
            mid = k_ref[:, at : at + cols].astype(f32)
            w = [0.25 * lax.shift_left(1, face_ref[f, x, y : y + 1, :]).astype(f32) for f in range(6)]
            total = ((w[0] + w[1]) + (w[2] + w[3])) + (w[4] + w[5])
            down = before[:, y * cols : (y + 1) * cols] if x == 0 else k_ref[:, at - plane : at - plane + cols].astype(f32)
            up = after[:, y * cols : (y + 1) * cols] if x == 1 else k_ref[:, at + plane : at + plane + cols].astype(f32)
            out = w[0] * down + w[1] * up - total * mid
            if y > 0:
                out += w[2] * k_ref[:, at - cols : at].astype(f32)
            if y < rows - 1:
                out += w[3] * k_ref[:, at + cols : at + 2 * cols].astype(f32)
            out += jnp.where(lane == 0, 0.0, w[4]) * pltpu.roll(mid, 1, 1)
            out += jnp.where(lane == cols - 1, 0.0, w[5]) * pltpu.roll(mid, cols - 1, 1)
            base_s[:, at : at + cols] = mid + step_size * out
            lap_s[:, at : at + cols] = out.astype(bf16)
    base_ref[...] = base_s[pl.ds(pl.multiple_of(c_ref[1] * base_ref.shape[0], 8), base_ref.shape[0]), :]
    m_ref[...] = dot(u_ref[...], lap_s[...], 1, 1)


def main_body(tile, scale, first, *refs):
    if first:
        kt_ref, own_ref, oth_ref, v_ref, g_ref, ma_ref, mb_ref, core_ref, l_ref, ov_ref, w_s = refs
    else:
        kt_ref, own_ref, oth_ref, v_ref, g_ref, ma_ref, mb_ref, core_ref, old_ref, l_ref, ov_ref, w_s = refs
    step = pl.program_id(0)
    rank = v_ref.shape[0]

    @pl.when(step == 0)
    def _():
        ov_ref[...] = jnp.zeros_like(ov_ref) if first else old_ref[...]
        w = core_ref[...].astype(bf16).astype(f32) * 0.125 + scale * (ma_ref[...] + mb_ref[...])
        high = w.astype(bf16)
        w_s[:rank, :] = high
        w_s[rank:, :] = (w - high.astype(f32)).astype(bf16)

    v = v_ref[...]
    g = g_ref[...]
    acc = None
    cells = own_ref.shape[1]
    for u_ref, base in ((own_ref, 0), (oth_ref, cells)):
        for at in range(0, cells, tile):
            field = dot(kt_ref[base + at : base + at + tile, :], v, 1, 0)
            react = (field * (g - field * field)).astype(bf16)
            ov_ref[base + at : base + at + tile, :] += dot(react, v, 1, 1)
            part = dot(u_ref[:, at : at + tile], react, 1, 0)
            acc = part if acc is None else acc + part
    side = dot(w_s[...], v, 1, 0)
    l_ref[...] = (scale * acc + (side[:rank] + side[rank:])).astype(bf16)


def turn_body(ov_ref, own_ref, oth_ref):
    cells = own_ref.shape[1]
    own_ref[...] = ov_ref[:cells, :].T
    oth_ref[...] = ov_ref[cells:, :].T.astype(bf16)


def spread(x, axes, parts):
    wide = jnp.broadcast_to(x[None], (parts,) + x.shape)
    wide = wide.reshape((parts * x.shape[0],) + x.shape[1:])
    return lax.all_to_all(wide, axes, 0, 0, tiled=True)


def per_device(basis_u, basis_v, core_s, face_class, sample_class):
    narrow, depth_x, rows_y, cols_z = basis_u.shape
    rank = core_s.shape[0]
    n_samp, n_space = 8, 16
    cells = depth_x * rows_y * cols_z
    lanes, samp_rows = basis_v.shape
    half = samp_rows // 2
    width = half // CHUNKS
    cell_weight = rank / (cells * n_space)
    samp_weight = rank / (samp_rows * n_samp)
    core_at = lax.axis_index("c")
    samp_at = lax.axis_index(SAMP)
    where_at = jnp.stack([core_at, samp_at]).astype(jnp.int32)
    swap = [(0, 1), (1, 0)]

    u_own = spread(basis_u.reshape(narrow, cells), SAMP, n_samp)
    v_parts = []
    v_half = basis_v.reshape(lanes, 2, CHUNKS, width)
    for j in range(CHUNKS):
        pair = jnp.transpose(v_half[:, :, j], (1, 0, 2))
        v_parts.append(spread(pair.reshape(2 * lanes, width), SPACE, n_space // 2))
    u_oth = lax.ppermute(u_own, "c", swap)

    smem = pl.BlockSpec(memory_space=pltpu.SMEM)
    vm = pl.BlockSpec(memory_space=pltpu.VMEM)
    k_own, near, kt, send = pl.pallas_call(
        prep_body,
        in_specs=[smem, vm, vm, vm],
        out_shape=[
            jax.ShapeDtypeStruct((rank, cells), bf16),
            jax.ShapeDtypeStruct((rank, cells // 2), bf16),
            jax.ShapeDtypeStruct((2 * cells, rank), bf16),
            jax.ShapeDtypeStruct((rank, cells // 2), bf16),
        ],
    )(where_at, u_own, u_oth, core_s)
    chips = n_space // 2
    hops = [(2 * i + 1, 2 * i + 2) for i in range(chips - 1)] + [(2 * i + 2, 2 * i + 1) for i in range(chips - 1)]
    halo = lax.ppermute(send, SPACE, hops)
    base, m_own = pl.pallas_call(
        functools.partial(lap_body, rows_y, cols_z),
        in_specs=[smem] + [vm] * 5,
        out_shape=[jax.ShapeDtypeStruct((narrow, cells), f32), jax.ShapeDtypeStruct((rank, rank), f32)],
        scratch_shapes=[pltpu.VMEM((rank, cells), f32), pltpu.VMEM((rank, cells), bf16)],
    )(where_at, k_own, near, halo, face_class, u_own)
    m_oth = lax.ppermute(m_own, "c", swap)

    growth = 0.5 + 0.5 * lax.dynamic_slice_in_dim(sample_class, core_at * half, half, 0).astype(f32)
    growth = growth.reshape(CHUNKS, 1, width)
    block = min(1024, width)
    ov = None
    l_parts = []
    for j in range(CHUNKS):
        first = j == 0
        ins = [kt, u_own, u_oth, v_parts[j], growth[j], m_own, m_oth, core_s] + ([] if first else [ov])
        specs = [
            whole(kt.shape),
            whole(u_own.shape),
            whole(u_oth.shape),
            pl.BlockSpec((rank, block), lambda i: (0, i)),
            pl.BlockSpec((1, block), lambda i: (0, i)),
            whole((rank, rank)),
            whole((rank, rank)),
            whole((rank, rank)),
        ] + ([] if first else [whole((2 * cells, rank))])
        l_part, ov = call(
            functools.partial(main_body, 512, step_size * cell_weight, first),
            [((rank, width), bf16), ((2 * cells, rank), f32)],
            grid=(width // block,),
            in_specs=specs,
            out_specs=[pl.BlockSpec((rank, block), lambda i: (0, i)), whole((2 * cells, rank))],
            scratch_shapes=[pltpu.VMEM((2 * rank, rank), bf16)],
        )(*ins)
        got = lax.all_to_all(l_part, SPACE, 0, 0, tiled=True)
        l_parts.append(got.reshape(n_space // 2, 2, lanes, width).astype(f32).sum(0))
    l_new = jnp.stack(l_parts, 2)
    l_new = jnp.transpose(l_new, (1, 0, 2, 3)).reshape(lanes, samp_rows)

    ov_own, ov_send = call(turn_body, [((rank, cells), f32), ((rank, cells), bf16)])(ov)
    ov_sum = (ov_own + lax.ppermute(ov_send, "c", swap).astype(f32)).astype(bf16)
    k_got = lax.all_to_all(ov_sum, SAMP, 0, 0, tiled=True)
    k_sum = k_got.reshape(n_samp, narrow, cells).astype(f32).sum(0)
    k_new = base + (step_size * samp_weight) * k_sum
    return (k_new.reshape(basis_u.shape), l_new)


def solution(mesh):
    fine = Mesh(mesh.devices.reshape(4, 2, 2, 4, 2), SPACE + SAMP)
    return jax.shard_map(
        per_device,
        mesh=fine,
        in_specs=(P(SAMP, SPACE, None, None), P(SPACE, SAMP), P(), P(None, SPACE, None, None), P(SAMP)),
        out_specs=(P(SAMP, SPACE, None, None), P(SPACE, SAMP)),
        check_vma=False,
    )
```

```python
import functools

import jax
import jax.numpy as jnp
from jax import lax
from jax.experimental import pallas as pl
from jax.experimental.pallas import tpu as pltpu
from jax.sharding import Mesh, PartitionSpec as P

step_size = 0.1
SPACE = ("z", "xl", "c")
SAMP = ("y", "xh")
bf16, f32 = jnp.bfloat16, jnp.float32


def dot(a, b, ca, cb):
    return lax.dot_general(a, b, (((ca,), (cb,)), ((), ())), preferred_element_type=f32)


def whole(shape):
    return pl.BlockSpec(shape, lambda *_: (0,) * len(shape))


def call(body, outs, grid=None, in_specs=None, out_specs=None, **kw):
    extra = {}
    if grid is not None:
        extra = dict(grid=grid, in_specs=in_specs, out_specs=out_specs)
    return pl.pallas_call(
        body,
        out_shape=[jax.ShapeDtypeStruct(s, d) for s, d in outs],
        compiler_params=pltpu.CompilerParams(vmem_limit_bytes=56 << 20),
        **extra,
        **kw,
    )


def fan_body(v_ref, out_ref):
    half = out_ref.shape[-1]
    for k in range(out_ref.shape[0]):
        out_ref[k, 0] = v_ref[:, :half]
        out_ref[k, 1] = v_ref[:, half:]


def prep_body(at_ref, u_ref, w_ref, a_ref, b_ref, c0_ref, c1_ref, core_ref, full_ref, k_ref, kt_ref, halo_ref):
    narrow, cells = u_ref.shape
    half = cells // 2
    y, xh = at_ref[2], at_ref[3]

    def put(turn, flip, value, start=0):
        row = (((y + turn) % 4) * 2 + (xh if flip == 0 else 1 - xh)) * narrow
        full_ref[pl.ds(pl.multiple_of(row, narrow), narrow), start : start + value.shape[1]] = value

    put(0, 0, u_ref[...])
    put(0, 1, w_ref[...])
    for turn, ref, start in ((3, a_ref, 0), (1, b_ref, 0), (2, c0_ref, 0), (2, c1_ref, half)):
        put(turn, 0, ref[:narrow, :], start)
        put(turn, 1, ref[narrow:, :], start)
    k_own = dot(core_ref[...].astype(bf16), full_ref[...], 0, 0).astype(bf16)
    k_ref[...] = k_own
    kt_ref[...] = k_own.T
    first = at_ref[0] == 0

    @pl.when(first)
    def _():
        halo_ref[...] = k_own[:, :half]

    @pl.when(jnp.logical_not(first))
    def _():
        halo_ref[...] = k_own[:, half:]


def other_body(at_ref, oth_ref, core_ref, kt_ref, near_ref):
    half = oth_ref.shape[1] // 2
    k_oth = dot(core_ref[...].astype(bf16), oth_ref[...], 0, 0).astype(bf16)
    kt_ref[...] = k_oth.T
    first = at_ref[0] == 0

    @pl.when(first)
    def _():
        near_ref[...] = k_oth[:, :half]

    @pl.when(jnp.logical_not(first))
    def _():
        near_ref[...] = k_oth[:, half:]


def lap_body(rows, cols, c_ref, k_ref, near_ref, halo_ref, face_ref, u_ref, base_ref, m_ref, base_s, lap_s):
    first = c_ref[0] == 0
    near = near_ref[...].astype(f32)
    halo = halo_ref[...].astype(f32)
    before = jnp.where(first, halo, near)
    after = jnp.where(first, near, halo)
    plane = rows * cols
    lane = lax.broadcasted_iota(jnp.int32, (1, cols), 1)
    for x in range(2):
        for y in range(rows):
            at = (x * rows + y) * cols
            mid = k_ref[:, at : at + cols].astype(f32)
            w = [0.25 * lax.shift_left(1, face_ref[f, x, y : y + 1, :]).astype(f32) for f in range(6)]
            total = ((w[0] + w[1]) + (w[2] + w[3])) + (w[4] + w[5])
            down = before[:, y * cols : (y + 1) * cols] if x == 0 else k_ref[:, at - plane : at - plane + cols].astype(f32)
            up = after[:, y * cols : (y + 1) * cols] if x == 1 else k_ref[:, at + plane : at + plane + cols].astype(f32)
            out = w[0] * down + w[1] * up - total * mid
            if y > 0:
                out += w[2] * k_ref[:, at - cols : at].astype(f32)
            if y < rows - 1:
                out += w[3] * k_ref[:, at + cols : at + 2 * cols].astype(f32)
            out += jnp.where(lane == 0, 0.0, w[4]) * pltpu.roll(mid, 1, 1)
            out += jnp.where(lane == cols - 1, 0.0, w[5]) * pltpu.roll(mid, cols - 1, 1)
            base_s[:, at : at + cols] = mid + step_size * out
            lap_s[:, at : at + cols] = out.astype(bf16)
    base_ref[...] = base_s[pl.ds(pl.multiple_of(c_ref[1] * base_ref.shape[0], 8), base_ref.shape[0]), :]
    m_ref[...] = dot(u_ref[...], lap_s[...], 1, 1)


def tile_sums(tile, kt_ref, u_ref, v, g, ov_ref):
    acc = None
    for at in range(0, u_ref.shape[1], tile):
        field = dot(kt_ref[at : at + tile, :], v, 1, 0)
        react = (field * (g - field * field)).astype(bf16)
        ov_ref[at : at + tile, :] += dot(react, v, 1, 1)
        part = dot(u_ref[:, at : at + tile], react, 1, 0)
        acc = part if acc is None else acc + part
    return acc


def own_body(tile, kt_ref, u_ref, v_ref, g_ref, l_ref, ov_ref):
    @pl.when(pl.program_id(0) == 0)
    def _():
        ov_ref[...] = jnp.zeros_like(ov_ref)

    l_ref[...] = tile_sums(tile, kt_ref, u_ref, v_ref[...], g_ref[...], ov_ref)


def oth_body(tile, scale, kt_ref, u_ref, v_ref, g_ref, old_ref, ma_ref, mb_ref, core_ref, l_ref, send_ref, w_s, ov_s):
    step = pl.program_id(0)
    rank = v_ref.shape[0]

    @pl.when(step == 0)
    def _():
        ov_s[...] = jnp.zeros_like(ov_s)
        w = core_ref[...].astype(bf16).astype(f32) * 0.125 + scale * (ma_ref[...] + mb_ref[...])
        high = w.astype(bf16)
        w_s[:rank, :] = high
        w_s[rank:, :] = (w - high.astype(f32)).astype(bf16)

    v = v_ref[...]
    acc = old_ref[...] + tile_sums(tile, kt_ref, u_ref, v, g_ref[...], ov_s)
    side = dot(w_s[...], v, 1, 0)
    l_ref[...] = (scale * acc + (side[:rank] + side[rank:])).astype(bf16)

    @pl.when(step == pl.num_programs(0) - 1)
    def _():
        send_ref[...] = ov_s[...].T.astype(bf16)


def turn_body(at_ref, ov_ref, got_ref, me_ref, up_ref, dn_ref, ol_ref, or_ref, tot_s):
    rows, cells = me_ref.shape
    half = cells // 2
    tot_s[...] = ov_ref[...].T + got_ref[...].astype(f32)
    y = at_ref[2]

    def part(turn):
        return tot_s[pl.ds(pl.multiple_of(((y + turn) % 4) * rows, rows), rows), :]

    me_ref[...] = part(0)
    up_ref[...] = part(1)
    dn_ref[...] = part(3)
    away = part(2).astype(bf16)
    ol_ref[...] = away[:, :half]
    or_ref[...] = away[:, half:]


def pass_body(up_ref, dn_ref, ra_ref, rb_ref, ou_ref, od_ref):
    half = ra_ref.shape[1]
    ou_ref[:, :half] = (up_ref[:, :half] + ra_ref[...].astype(f32)).astype(bf16)
    ou_ref[:, half:] = up_ref[:, half:].astype(bf16)
    od_ref[:, :half] = dn_ref[:, :half].astype(bf16)
    od_ref[:, half:] = (dn_ref[:, half:] + rb_ref[...].astype(f32)).astype(bf16)


def pair_body(at_ref, me_ref, rc_ref, rd_ref, mine_ref, send_ref, tot_s):
    rows = mine_ref.shape[0]
    tot_s[...] = me_ref[...] + rc_ref[...].astype(f32) + rd_ref[...].astype(f32)
    xh = at_ref[3]
    mine_ref[...] = tot_s[pl.ds(pl.multiple_of(xh * rows, rows), rows), :]
    send_ref[...] = tot_s[pl.ds(pl.multiple_of((1 - xh) * rows, rows), rows), :].astype(bf16)


def ring(n, k):
    return [(i, (i + k) % n) for i in range(n)]


def small(body, n_in, outs, scratch=(), scalars=True):
    vm = pl.BlockSpec(memory_space=pltpu.VMEM)
    return pl.pallas_call(
        body,
        in_specs=([pl.BlockSpec(memory_space=pltpu.SMEM)] if scalars else []) + [vm] * n_in,
        out_specs=[vm] * len(outs),
        out_shape=[jax.ShapeDtypeStruct(s, d) for s, d in outs],
        scratch_shapes=[pltpu.VMEM(s, d) for s, d in scratch],
        compiler_params=pltpu.CompilerParams(vmem_limit_bytes=56 << 20),
    )


def per_device(basis_u, basis_v, core_s, face_class, sample_class):
    narrow, depth_x, rows_y, cols_z = basis_u.shape
    rank = core_s.shape[0]
    n_samp, n_space = 8, 16
    cells = depth_x * rows_y * cols_z
    lanes, samp_rows = basis_v.shape
    half = samp_rows // 2
    cell_weight = rank / (cells * n_space)
    samp_weight = rank / (samp_rows * n_samp)
    core_at = lax.axis_index("c")
    where_at = jnp.stack([core_at, lax.axis_index(SAMP), lax.axis_index("y"), lax.axis_index("xh")]).astype(jnp.int32)
    swap = ring(2, 1)

    (v_wide,) = small(fan_body, 1, [((n_space // 2, 2, lanes, half), bf16)], scalars=False)(basis_v)
    v = lax.all_to_all(v_wide.reshape(rank, half), SPACE, 0, 0, tiled=True)
    u0 = basis_u.reshape(narrow, cells)
    u1 = lax.ppermute(u0, "xh", swap)
    pair = jnp.concatenate([u0, u1], 0)
    ua = lax.ppermute(pair, "y", ring(4, 1))
    ub = lax.ppermute(pair, "y", ring(4, 3))
    uc = lax.ppermute(ua[:, : cells // 2], "y", ring(4, 1))
    ud = lax.ppermute(ub[:, cells // 2 :], "y", ring(4, 3))
    u_own, k_own, kt_own, edge = small(
        prep_body,
        7,
        [((rank, cells), bf16), ((rank, cells), bf16), ((cells, rank), bf16), ((rank, cells // 2), bf16)],
    )(where_at, u0, u1, ua, ub, uc, ud, core_s)
    u_oth = lax.ppermute(u_own, "c", swap)
    chips = n_space // 2
    hops = [(2 * i + 1, 2 * i + 2) for i in range(chips - 1)] + [(2 * i + 2, 2 * i + 1) for i in range(chips - 1)]
    halo = lax.ppermute(edge, SPACE, hops)

    growth = 0.5 + 0.5 * lax.dynamic_slice_in_dim(sample_class, core_at * half, half, 0).astype(f32)
    growth = growth.reshape(1, half)
    block, tile = 1024, 512
    steps = half // block
    by_sample = lambda n: pl.BlockSpec((n, block), lambda i: (0, i))
    l_own, ov_own = call(
        functools.partial(own_body, tile),
        [((rank, half), f32), ((cells, rank), f32)],
        grid=(steps,),
        in_specs=[whole((cells, rank)), whole((rank, cells)), by_sample(rank), by_sample(1)],
        out_specs=[by_sample(rank), whole((cells, rank))],
    )(kt_own, u_own, v, growth)

    kt_oth, near = small(other_body, 2, [((cells, rank), bf16), ((rank, cells // 2), bf16)])(where_at, u_oth, core_s)
    base, m_own = small(
        functools.partial(lap_body, rows_y, cols_z),
        5,
        [((narrow, cells), f32), ((rank, rank), f32)],
        [((rank, cells), f32), ((rank, cells), bf16)],
    )(where_at, k_own, near, halo, face_class, u_own)
    m_oth = lax.ppermute(m_own, "c", swap)

    l_part, ov_send = call(
        functools.partial(oth_body, tile, step_size * cell_weight),
        [((rank, half), bf16), ((rank, cells), bf16)],
        grid=(steps,),
        in_specs=[whole((cells, rank)), whole((rank, cells)), by_sample(rank), by_sample(1), by_sample(rank)]
        + [whole((rank, rank))] * 3,
        out_specs=[by_sample(rank), whole((rank, cells))],
        scratch_shapes=[pltpu.VMEM((2 * rank, rank), bf16), pltpu.VMEM((cells, rank), f32)],
    )(kt_oth, u_oth, v, growth, l_own, m_own, m_oth, core_s)

    l_got = lax.all_to_all(l_part, SPACE, 0, 0, tiled=True)
    l_new = l_got.reshape(n_space // 2, 2, lanes, half).astype(f32).sum(0)
    l_new = jnp.transpose(l_new, (1, 0, 2)).reshape(lanes, samp_rows)

    got = lax.ppermute(ov_send, "c", swap)
    rows = rank // 4
    me, up, dn, away_l, away_r = small(
        turn_body, 2, [((rows, cells), f32)] * 3 + [((rows, cells // 2), bf16)] * 2, [((rank, cells), f32)]
    )(where_at, ov_own, got)
    ra = lax.ppermute(away_l, "y", ring(4, 1))
    rb = lax.ppermute(away_r, "y", ring(4, 3))
    out_u, out_d = small(pass_body, 4, [((rows, cells), bf16)] * 2, scalars=False)(up, dn, ra, rb)
    rc = lax.ppermute(out_u, "y", ring(4, 1))
    rd = lax.ppermute(out_d, "y", ring(4, 3))
    mine, send = small(pair_body, 3, [((narrow, cells), f32), ((narrow, cells), bf16)], [((rows, cells), f32)])(
        where_at, me, rc, rd
    )
    k_sum = mine + lax.ppermute(send, "xh", swap).astype(f32)
    k_new = base + (step_size * samp_weight) * k_sum
    return (k_new.reshape(basis_u.shape), l_new)


def solution(mesh):
    fine = Mesh(mesh.devices.reshape(4, 2, 2, 4, 2), SPACE + SAMP)
    return jax.shard_map(
        per_device,
        mesh=fine,
        in_specs=(P(SAMP, SPACE, None, None), P(SPACE, SAMP), P(), P(None, SPACE, None, None), P(SAMP)),
        out_specs=(P(SAMP, SPACE, None, None), P(SPACE, SAMP)),
        check_vma=False,
    )
```

```python
import functools

import jax
import jax.numpy as jnp
from jax import lax
from jax.experimental import pallas as pl
from jax.experimental.pallas import tpu as pltpu
from jax.sharding import Mesh, PartitionSpec as P

step_size = 0.1
SPACE = ("z", "xl", "c")
SAMP = ("y", "xh")
bf16, f32 = jnp.bfloat16, jnp.float32


def dot(a, b, ca, cb):
    return lax.dot_general(a, b, (((ca,), (cb,)), ((), ())), preferred_element_type=f32)


def resident(x):
    return pltpu.with_memory_space_constraint(x, pltpu.MemorySpace.VMEM)


def small(body, args, outs, scratch=(), at=None, after=(), limit=24):
    vm = pl.BlockSpec(memory_space=pltpu.VMEM)
    scalars = [] if at is None else [at]
    return pl.pallas_call(
        body,
        in_specs=[pl.BlockSpec(memory_space=pltpu.SMEM)] * len(scalars)
        + [vm] * len(args)
        + [pl.BlockSpec(memory_space=pl.ANY)] * len(after),
        out_specs=[vm] * len(outs),
        out_shape=[pltpu.VMEM(shape, dtype) if keep else jax.ShapeDtypeStruct(shape, dtype) for shape, dtype, keep in outs],
        scratch_shapes=[pltpu.VMEM(shape, dtype) for shape, dtype in scratch],
        compiler_params=pltpu.CompilerParams(vmem_limit_bytes=limit << 20),
    )(*scalars, *args, *after)


def fan_body(v_ref, out_ref):
    half = out_ref.shape[-1]
    for k in range(out_ref.shape[0]):
        out_ref[k, 0] = v_ref[:, :half]
        out_ref[k, 1] = v_ref[:, half:]


def prep_body(at_ref, u_ref, w_ref, a_ref, b_ref, c_ref, core_ref, full_ref, k_ref, kt_ref, halo_ref):
    narrow, cells = u_ref.shape
    half = cells // 2
    y, xh = at_ref[2], at_ref[3]

    def put(turn, flip, value):
        row = (((y + turn) % 4) * 2 + (xh if flip == 0 else 1 - xh)) * narrow
        full_ref[pl.ds(pl.multiple_of(row, narrow), narrow), :] = value

    put(0, 0, u_ref[...])
    put(0, 1, w_ref[...])
    for turn, ref in ((3, a_ref), (1, b_ref), (2, c_ref)):
        put(turn, 0, ref[:narrow, :])
        put(turn, 1, ref[narrow:, :])
    k_own = dot(core_ref[...].astype(bf16), full_ref[...], 0, 0).astype(bf16)
    k_ref[...] = k_own
    kt_ref[...] = k_own.T
    first = at_ref[0] == 0

    @pl.when(first)
    def _():
        halo_ref[...] = k_own[:, :half]

    @pl.when(jnp.logical_not(first))
    def _():
        halo_ref[...] = k_own[:, half:]


def mid_body(rows, cols, c_ref, oth_ref, core_ref, k_ref, halo_ref, face_ref, u_ref, after_ref, kt_ref, base_ref, m_ref, base_s, lap_s):
    half = oth_ref.shape[1] // 2
    k_oth = dot(core_ref[...].astype(bf16), oth_ref[...], 0, 0).astype(bf16)
    kt_ref[...] = k_oth.T
    first = c_ref[0] == 0
    near = jnp.where(first, k_oth[:, :half].astype(f32), k_oth[:, half:].astype(f32))
    halo = halo_ref[...].astype(f32)
    before = jnp.where(first, halo, near)
    after = jnp.where(first, near, halo)
    plane = rows * cols
    lane = lax.broadcasted_iota(jnp.int32, (1, cols), 1)
    for x in range(2):
        for y in range(rows):
            at = (x * rows + y) * cols
            mid = k_ref[:, at : at + cols].astype(f32)
            w = [0.25 * lax.shift_left(1, face_ref[f, x, y : y + 1, :]).astype(f32) for f in range(6)]
            total = ((w[0] + w[1]) + (w[2] + w[3])) + (w[4] + w[5])
            down = before[:, y * cols : (y + 1) * cols] if x == 0 else k_ref[:, at - plane : at - plane + cols].astype(f32)
            up = after[:, y * cols : (y + 1) * cols] if x == 1 else k_ref[:, at + plane : at + plane + cols].astype(f32)
            out = w[0] * down + w[1] * up - total * mid
            if y > 0:
                out += w[2] * k_ref[:, at - cols : at].astype(f32)
            if y < rows - 1:
                out += w[3] * k_ref[:, at + cols : at + 2 * cols].astype(f32)
            out += jnp.where(lane == 0, 0.0, w[4]) * pltpu.roll(mid, 1, 1)
            out += jnp.where(lane == cols - 1, 0.0, w[5]) * pltpu.roll(mid, cols - 1, 1)
            base_s[:, at : at + cols] = mid + step_size * out
            lap_s[:, at : at + cols] = out.astype(bf16)
    base_ref[...] = base_s[pl.ds(pl.multiple_of(c_ref[1] * base_ref.shape[0], 8), base_ref.shape[0]), :]
    m_ref[...] = dot(u_ref[...], lap_s[...], 1, 1)


def sweep(kt_ref, u_ref, v_ref, g_ref, ov_ref, start, store, block=1024, tile=512):
    def turn(i, _):
        at = pl.multiple_of(start + i * block, block)
        v = v_ref[:, pl.ds(at, block)]
        g = g_ref[:, pl.ds(at, block)]
        acc = None
        for row in range(0, u_ref.shape[1], tile):
            field = dot(kt_ref[row : row + tile, :], v, 1, 0)
            react = (field * (g - field * field)).astype(bf16)
            ov_ref[row : row + tile, :] += dot(react, v, 1, 1)
            part = dot(u_ref[:, row : row + tile], react, 1, 0)
            acc = part if acc is None else acc + part
        store(at, acc, v)
        return 0

    return turn


def own_body(kt_ref, u_ref, v_ref, g_ref, l_ref, ov_ref):
    ov_ref[...] = jnp.zeros_like(ov_ref)

    def store(at, acc, v):
        l_ref[:, pl.ds(at, acc.shape[1])] = acc

    lax.fori_loop(0, l_ref.shape[1] // 1024, sweep(kt_ref, u_ref, v_ref, g_ref, ov_ref, 0, store), 0)


def oth_body(scale, kt_ref, u_ref, v_ref, g_ref, old_ref, ma_ref, mb_ref, core_ref, l_ref, send_ref, w_s, ov_s):
    rank = v_ref.shape[0]
    ov_s[...] = jnp.zeros_like(ov_s)
    w = core_ref[...].astype(bf16).astype(f32) * 0.125 + scale * (ma_ref[...] + mb_ref[...])
    high = w.astype(bf16)
    w_s[:rank, :] = high
    w_s[rank:, :] = (w - high.astype(f32)).astype(bf16)

    def store(at, acc, v):
        side = dot(w_s[...], v, 1, 0)
        l_ref[:, pl.ds(at, acc.shape[1])] = scale * acc + (side[:rank] + side[rank:])

    lax.fori_loop(0, l_ref.shape[1] // 1024, sweep(kt_ref, u_ref, v_ref, g_ref, ov_s, 0, store), 0)
    done = old_ref.shape[1]
    l_ref[:, :done] += scale * old_ref[...]
    send_ref[...] = ov_s[...].T.astype(bf16)


def last_body(scale, at_ref, kt_ref, u_ref, v_ref, g_ref, l_ref, ov_ref, got_ref, out_ref, me_ref, up_ref, dn_ref, away_ref, ov_s, tot_s):
    half = v_ref.shape[1] // 2
    ov_s[...] = ov_ref[...]
    out_ref[:, :half] = l_ref[:, :half].astype(bf16)

    def store(at, acc, v):
        here = pl.ds(at, acc.shape[1])
        out_ref[:, here] = (l_ref[:, here] + scale * acc).astype(bf16)

    lax.fori_loop(0, half // 1024, sweep(kt_ref, u_ref, v_ref, g_ref, ov_s, half, store), 0)
    tot_s[...] = ov_s[...].T + got_ref[...].astype(f32)
    rows = me_ref.shape[0]
    y = at_ref[2]

    def part(turn):
        return tot_s[pl.ds(pl.multiple_of(((y + turn) % 4) * rows, rows), rows), :]

    me_ref[...] = part(0)
    up_ref[...] = part(1).astype(bf16)
    away_ref[...] = part(2).astype(bf16)
    dn_ref[...] = part(3).astype(bf16)


def pair_body(at_ref, me_ref, rc_ref, rd_ref, re_ref, mine_ref, send_ref, tot_s):
    rows = mine_ref.shape[0]
    tot_s[...] = (me_ref[...] + rc_ref[...].astype(f32)) + (rd_ref[...].astype(f32) + re_ref[...].astype(f32))
    xh = at_ref[3]
    mine_ref[...] = tot_s[pl.ds(pl.multiple_of(xh * rows, rows), rows), :]
    send_ref[...] = tot_s[pl.ds(pl.multiple_of((1 - xh) * rows, rows), rows), :].astype(bf16)


def ring(n, k):
    return [(i, (i + k) % n) for i in range(n)]


def per_device(basis_u, basis_v, core_s, face_class, sample_class):
    narrow, depth_x, rows_y, cols_z = basis_u.shape
    rank = core_s.shape[0]
    n_samp, n_space = 8, 16
    cells = depth_x * rows_y * cols_z
    lanes, samp_rows = basis_v.shape
    half = samp_rows // 2
    cell_weight = rank / (cells * n_space)
    samp_weight = rank / (samp_rows * n_samp)
    core_at = lax.axis_index("c")
    where_at = jnp.stack([core_at, lax.axis_index(SAMP), lax.axis_index("y"), lax.axis_index("xh")]).astype(jnp.int32)
    swap = ring(2, 1)

    (v_wide,) = small(fan_body, [basis_v], [((n_space // 2, 2, lanes, half), bf16, False)])
    v = resident(lax.all_to_all(v_wide.reshape(rank, half), SPACE, 0, 0, tiled=True))
    u0 = basis_u.reshape(narrow, cells)
    u1 = lax.ppermute(u0, "xh", swap)
    pair = jnp.concatenate([u0, u1], 0)
    around = [resident(lax.ppermute(pair, "y", ring(4, k))) for k in (1, 3, 2)]
    u_own, k_own, kt_own, edge = small(
        prep_body,
        [resident(u0), resident(u1), *around, core_s],
        [((rank, cells), bf16, True), ((rank, cells), bf16, True), ((cells, rank), bf16, True), ((rank, cells // 2), bf16, True)],
        at=where_at,
    )
    u_oth = resident(lax.ppermute(u_own, "c", swap))
    chips = n_space // 2
    hops = [(2 * i + 1, 2 * i + 2) for i in range(chips - 1)] + [(2 * i + 2, 2 * i + 1) for i in range(chips - 1)]
    halo = resident(lax.ppermute(edge, SPACE, hops))

    growth = 0.5 + 0.5 * lax.dynamic_slice_in_dim(sample_class, core_at * half, half, 0).astype(f32)
    growth = resident(growth.reshape(1, half))
    scale = step_size * cell_weight
    l_first, ov_first = small(
        own_body, [kt_own, u_own, v, growth], [((rank, half // 2), f32, True), ((cells, rank), f32, True)]
    )
    kt_oth, base, m_own = small(
        functools.partial(mid_body, rows_y, cols_z),
        [u_oth, core_s, k_own, halo, face_class, u_own],
        [((cells, rank), bf16, True), ((narrow, cells), f32, True), ((rank, rank), f32, True)],
        [((rank, cells), f32), ((rank, cells), bf16)],
        at=where_at,
        after=(ov_first,),
    )
    m_oth = resident(lax.ppermute(m_own, "c", swap))
    l_most, ov_send = small(
        functools.partial(oth_body, scale),
        [kt_oth, u_oth, v, growth, l_first, m_own, m_oth, core_s],
        [((rank, half), f32, True), ((rank, cells), bf16, True)],
        [((2 * rank, rank), bf16), ((cells, rank), f32)],
    )
    got = resident(lax.ppermute(ov_send, "c", swap))
    rows = rank // 4
    l_part, me, up, dn, away = small(
        functools.partial(last_body, scale),
        [kt_own, u_own, v, growth, l_most, ov_first, got],
        [((rank, half), bf16, False), ((rows, cells), f32, True)] + [((rows, cells), bf16, True)] * 3,
        [((cells, rank), f32), ((rank, cells), f32)],
        at=where_at,
    )

    l_got = lax.all_to_all(l_part, SPACE, 0, 0, tiled=True)
    l_new = l_got.reshape(n_space // 2, 2, lanes, half).astype(f32).sum(0)
    l_new = jnp.transpose(l_new, (1, 0, 2)).reshape(lanes, samp_rows)

    near = [resident(lax.ppermute(part, "y", ring(4, k))) for part, k in ((up, 1), (dn, 3), (away, 2))]
    mine, send = small(
        pair_body,
        [me, *near],
        [((narrow, cells), f32, True), ((narrow, cells), bf16, True)],
        [((rows, cells), f32)],
        at=where_at,
    )
    k_sum = mine + lax.ppermute(send, "xh", swap).astype(f32)
    k_new = base + (step_size * samp_weight) * k_sum
    return (k_new.reshape(basis_u.shape), l_new)


def solution(mesh):
    fine = Mesh(mesh.devices.reshape(4, 2, 2, 4, 2), SPACE + SAMP)
    return jax.shard_map(
        per_device,
        mesh=fine,
        in_specs=(P(SAMP, SPACE, None, None), P(SPACE, SAMP), P(), P(None, SPACE, None, None), P(SAMP)),
        out_specs=(P(SAMP, SPACE, None, None), P(SPACE, SAMP)),
        check_vma=False,
    )
```

```python
import functools

import jax
import jax.numpy as jnp
from jax import lax
from jax.experimental import pallas as pl
from jax.experimental.pallas import tpu as pltpu
from jax.sharding import Mesh, PartitionSpec as P

step_size = 0.1
SPACE = ("z", "xl", "c")
SAMP = ("y", "xh")
bf16, f32 = jnp.bfloat16, jnp.float32


def dot(a, b, ca, cb):
    return lax.dot_general(a, b, (((ca,), (cb,)), ((), ())), preferred_element_type=f32)


def resident(x):
    return pltpu.with_memory_space_constraint(x, pltpu.MemorySpace.VMEM)


def small(body, args, outs, scratch=(), at=None, after=(), held=(), limit=24):
    vm = pl.BlockSpec(memory_space=pltpu.VMEM)
    scalars = [] if at is None else [at]
    n_read = len(scalars) + len(args)
    n_skip = len(held) + len(after)

    def reading(*refs):
        body(*refs[:n_read], *refs[n_read + n_skip :])

    return pl.pallas_call(
        reading,
        in_specs=[pl.BlockSpec(memory_space=pltpu.SMEM)] * len(scalars)
        + [vm] * (len(args) + len(held))
        + [pl.BlockSpec(memory_space=pl.ANY)] * len(after),
        out_specs=[vm] * len(outs),
        out_shape=[(pltpu.VMEM if keep else pltpu.HBM)(shape, dtype) for shape, dtype, keep in outs],
        scratch_shapes=[pltpu.VMEM(shape, dtype) for shape, dtype in scratch],
        compiler_params=pltpu.CompilerParams(vmem_limit_bytes=limit << 20),
    )(*scalars, *args, *held, *after)


def fan_body(v_ref, out_ref, sems):
    chips, parts, _, half = out_ref.shape
    copies = [
        pltpu.make_async_copy(v_ref.at[:, p * half : (p + 1) * half], out_ref.at[k, p], sems.at[k * parts + p])
        for k in range(chips)
        for p in range(parts)
    ]
    for copy in copies:
        copy.start()
    for copy in copies:
        copy.wait()


def prep_body(at_ref, u_ref, w_ref, a_ref, b_ref, c_ref, core_ref, full_ref, k_ref, kt_ref, halo_ref):
    narrow, cells = u_ref.shape
    half = cells // 2
    y, xh = at_ref[2], at_ref[3]

    def put(turn, flip, value):
        row = (((y + turn) % 4) * 2 + (xh if flip == 0 else 1 - xh)) * narrow
        full_ref[pl.ds(pl.multiple_of(row, narrow), narrow), :] = value

    put(0, 0, u_ref[...])
    put(0, 1, w_ref[...])
    for turn, ref in ((3, a_ref), (1, b_ref), (2, c_ref)):
        put(turn, 0, ref[:narrow, :])
        put(turn, 1, ref[narrow:, :])
    k_own = dot(core_ref[...].astype(bf16), full_ref[...], 0, 0).astype(bf16)
    k_ref[...] = k_own
    kt_ref[...] = k_own.T
    first = at_ref[0] == 0

    @pl.when(first)
    def _():
        halo_ref[...] = k_own[:, :half]

    @pl.when(jnp.logical_not(first))
    def _():
        halo_ref[...] = k_own[:, half:]


def mid_body(rows, cols, c_ref, oth_ref, core_ref, k_ref, halo_ref, face_ref, u_ref, kt_ref, base_ref, m_ref, base_s, lap_s):
    half = oth_ref.shape[1] // 2
    k_oth = dot(core_ref[...].astype(bf16), oth_ref[...], 0, 0).astype(bf16)
    kt_ref[...] = k_oth.T
    first = c_ref[0] == 0
    near = jnp.where(first, k_oth[:, :half].astype(f32), k_oth[:, half:].astype(f32))
    halo = halo_ref[...].astype(f32)
    before = jnp.where(first, halo, near)
    after = jnp.where(first, near, halo)
    plane = rows * cols
    lane = lax.broadcasted_iota(jnp.int32, (1, cols), 1)
    for x in range(2):
        for y in range(rows):
            at = (x * rows + y) * cols
            mid = k_ref[:, at : at + cols].astype(f32)
            w = [0.25 * lax.shift_left(1, face_ref[f, x, y : y + 1, :]).astype(f32) for f in range(6)]
            total = ((w[0] + w[1]) + (w[2] + w[3])) + (w[4] + w[5])
            down = before[:, y * cols : (y + 1) * cols] if x == 0 else k_ref[:, at - plane : at - plane + cols].astype(f32)
            up = after[:, y * cols : (y + 1) * cols] if x == 1 else k_ref[:, at + plane : at + plane + cols].astype(f32)
            out = w[0] * down + w[1] * up - total * mid
            if y > 0:
                out += w[2] * k_ref[:, at - cols : at].astype(f32)
            if y < rows - 1:
                out += w[3] * k_ref[:, at + cols : at + 2 * cols].astype(f32)
            out += jnp.where(lane == 0, 0.0, w[4]) * pltpu.roll(mid, 1, 1)
            out += jnp.where(lane == cols - 1, 0.0, w[5]) * pltpu.roll(mid, cols - 1, 1)
            base_s[:, at : at + cols] = mid + step_size * out
            lap_s[:, at : at + cols] = out.astype(bf16)
    base_ref[...] = base_s[pl.ds(pl.multiple_of(c_ref[1] * base_ref.shape[0], 8), base_ref.shape[0]), :]
    m_ref[...] = dot(u_ref[...], lap_s[...], 1, 1)


def sweep(kt_ref, u_ref, v_ref, g_ref, ov_ref, start, store, tile=512):
    block = BLOCK

    def turn(i, _):
        at = pl.multiple_of(start + i * block, block)
        v = v_ref[:, pl.ds(at, block)]
        g = g_ref[:, pl.ds(at, block)]
        acc = None
        for row in range(0, u_ref.shape[1], tile):
            field = dot(kt_ref[row : row + tile, :], v, 1, 0)
            react = (field * (g - field * field)).astype(bf16)
            ov_ref[row : row + tile, :] += dot(react, v, 1, 1)
            part = dot(u_ref[:, row : row + tile], react, 1, 0)
            acc = part if acc is None else acc + part
        store(at, acc, v)
        return 0

    return turn


BLOCK = 2048


def own_body(kt_ref, u_ref, v_ref, g_ref, l_ref, ov_ref):
    ov_ref[...] = jnp.zeros_like(ov_ref)

    def store(at, acc, v):
        l_ref[:, pl.ds(at, acc.shape[1])] = acc

    lax.fori_loop(0, l_ref.shape[1] // BLOCK, sweep(kt_ref, u_ref, v_ref, g_ref, ov_ref, 0, store), 0)


def oth_body(kt_ref, u_ref, v_ref, g_ref, old_ref, l_ref, ov_ref):
    ov_ref[...] = jnp.zeros_like(ov_ref)

    def store(at, acc, v):
        here = pl.ds(at, acc.shape[1])
        l_ref[:, here] = old_ref[:, here] + acc

    lax.fori_loop(0, l_ref.shape[1] // BLOCK, sweep(kt_ref, u_ref, v_ref, g_ref, ov_ref, 0, store), 0)


def turn_body(scale, kt_ref, u_ref, v_ref, g_ref, old_ref, ov_ref, ma_ref, mb_ref, core_ref, sent_ref, l_ref, send_ref, w_s, ov_s):
    rank = v_ref.shape[0]
    half = l_ref.shape[1]
    ov_s[...] = ov_ref[...]
    w = core_ref[...].astype(bf16).astype(f32) * 0.125 + scale * (ma_ref[...] + mb_ref[...])
    high = w.astype(bf16)
    w_s[:rank, :] = high
    w_s[rank:, :] = (w - high.astype(f32)).astype(bf16)
    side = dot(w_s[...], v_ref[:, :half], 1, 0)
    sent_ref[...] = (scale * old_ref[...] + (side[:rank] + side[rank:])).astype(bf16)

    def store(at, acc, v):
        part = dot(w_s[...], v, 1, 0)
        l_ref[:, pl.ds(at - half, acc.shape[1])] = scale * acc + (part[:rank] + part[rank:])

    lax.fori_loop(0, half // BLOCK, sweep(kt_ref, u_ref, v_ref, g_ref, ov_s, half, store), 0)
    send_ref[...] = ov_s[...].T.astype(bf16)


def last_body(scale, at_ref, kt_ref, u_ref, v_ref, g_ref, l_ref, ov_ref, got_ref, out_ref, me_ref, up_ref, dn_ref, away_ref, ov_s, tot_s):
    half = out_ref.shape[1]
    ov_s[...] = ov_ref[...]

    def store(at, acc, v):
        here = pl.ds(at - half, acc.shape[1])
        out_ref[:, here] = (l_ref[:, here] + scale * acc).astype(bf16)

    lax.fori_loop(0, half // BLOCK, sweep(kt_ref, u_ref, v_ref, g_ref, ov_s, half, store), 0)
    tot_s[...] = ov_s[...].T + got_ref[...].astype(f32)
    rows = me_ref.shape[0]
    y = at_ref[2]

    def part(turn):
        return tot_s[pl.ds(pl.multiple_of(((y + turn) % 4) * rows, rows), rows), :]

    me_ref[...] = part(0)
    up_ref[...] = part(1).astype(bf16)
    away_ref[...] = part(2).astype(bf16)
    dn_ref[...] = part(3).astype(bf16)


def pair_body(at_ref, me_ref, rc_ref, rd_ref, re_ref, mine_ref, send_ref, tot_s):
    rows = mine_ref.shape[0]
    tot_s[...] = (me_ref[...] + rc_ref[...].astype(f32)) + (rd_ref[...].astype(f32) + re_ref[...].astype(f32))
    xh = at_ref[3]
    mine_ref[...] = tot_s[pl.ds(pl.multiple_of(xh * rows, rows), rows), :]
    send_ref[...] = tot_s[pl.ds(pl.multiple_of((1 - xh) * rows, rows), rows), :].astype(bf16)


def ring(n, k):
    return [(i, (i + k) % n) for i in range(n)]


def per_device(basis_u, basis_v, core_s, face_class, sample_class):
    narrow, depth_x, rows_y, cols_z = basis_u.shape
    rank = core_s.shape[0]
    n_samp, n_space = 8, 16
    cells = depth_x * rows_y * cols_z
    lanes, samp_rows = basis_v.shape
    half = samp_rows // 2
    cell_weight = rank / (cells * n_space)
    samp_weight = rank / (samp_rows * n_samp)
    core_at = lax.axis_index("c")
    where_at = jnp.stack([core_at, lax.axis_index(SAMP), lax.axis_index("y"), lax.axis_index("xh")]).astype(jnp.int32)
    swap = ring(2, 1)

    anywhere = pl.BlockSpec(memory_space=pl.ANY)
    v_wide = pl.pallas_call(
        fan_body,
        in_specs=[anywhere],
        out_specs=anywhere,
        out_shape=jax.ShapeDtypeStruct((n_space // 2, 2, lanes, half), bf16),
        scratch_shapes=[pltpu.SemaphoreType.DMA((n_space,))],
    )(basis_v)
    basis_u, v_wide = lax.optimization_barrier((basis_u, v_wide))
    v = resident(lax.all_to_all(v_wide.reshape(rank, half), SPACE, 0, 0, tiled=True))
    u0 = basis_u.reshape(narrow, cells)
    u1 = lax.ppermute(u0, "xh", swap)
    pair = jnp.concatenate([u0, u1], 0)
    around = [resident(lax.ppermute(pair, "y", ring(4, k))) for k in (1, 3, 2)]
    u_own, k_own, kt_own, edge = small(
        prep_body,
        [resident(u0), resident(u1), *around, core_s],
        [((rank, cells), bf16, True), ((rank, cells), bf16, True), ((cells, rank), bf16, True), ((rank, cells // 2), bf16, True)],
        at=where_at,
    )
    u_oth = resident(lax.ppermute(u_own, "c", swap))
    chips = n_space // 2
    hops = [(2 * i + 1, 2 * i + 2) for i in range(chips - 1)] + [(2 * i + 2, 2 * i + 1) for i in range(chips - 1)]
    halo = resident(lax.ppermute(edge, SPACE, hops))

    growth = 0.5 + 0.5 * lax.dynamic_slice_in_dim(sample_class, core_at * half, half, 0).astype(f32)
    growth = resident(growth.reshape(1, half))
    scale = step_size * cell_weight
    quart = half // 2
    l_first, ov_first = small(own_body, [kt_own, u_own, v, growth], [((rank, quart), f32, True), ((cells, rank), f32, True)])
    kt_oth, base, m_own = small(
        functools.partial(mid_body, rows_y, cols_z),
        [u_oth, core_s, k_own, halo, face_class, u_own],
        [((cells, rank), bf16, True), ((narrow, cells), f32, False), ((rank, rank), f32, True)],
        [((rank, cells), f32), ((rank, cells), bf16)],
        at=where_at,
        held=(ov_first, kt_own, l_first),
    )
    m_oth = resident(lax.ppermute(m_own, "c", swap))
    l_both, ov_oth = small(
        oth_body, [kt_oth, u_oth, v, growth, l_first], [((rank, quart), f32, True), ((cells, rank), f32, True)], held=(ov_first, kt_own, u_own)
    )
    l_sent0, l_rest, ov_send = small(
        functools.partial(turn_body, scale),
        [kt_oth, u_oth, v, growth, l_both, ov_oth, m_own, m_oth, core_s],
        [((rank, quart), bf16, False), ((rank, quart), f32, True), ((rank, cells), bf16, True)],
        [((2 * rank, rank), bf16), ((cells, rank), f32)],
        held=(ov_first, kt_own, u_own),
    )
    got = resident(lax.ppermute(ov_send, "c", swap))
    l_got0 = lax.all_to_all(l_sent0, SPACE, 0, 0, tiled=True)
    rows = rank // 4
    l_sent1, me, up, dn, away = small(
        functools.partial(last_body, scale),
        [kt_own, u_own, v, growth, l_rest, ov_first, got],
        [((rank, quart), bf16, False), ((rows, cells), f32, True)] + [((rows, cells), bf16, True)] * 3,
        [((cells, rank), f32), ((rank, cells), f32)],
        at=where_at,
    )

    l_got1 = lax.all_to_all(l_sent1, SPACE, 0, 0, tiled=True)
    l_new = [got.reshape(n_space // 2, 2, lanes, quart).astype(f32).sum(0) for got in (l_got0, l_got1)]
    l_new = jnp.transpose(jnp.stack(l_new, 2), (1, 0, 2, 3)).reshape(lanes, samp_rows)

    near = [resident(lax.ppermute(part, "y", ring(4, k))) for part, k in ((up, 1), (dn, 3), (away, 2))]
    mine, send = small(
        pair_body,
        [me, *near],
        [((narrow, cells), f32, True), ((narrow, cells), bf16, True)],
        [((rows, cells), f32)],
        at=where_at,
    )
    k_sum = mine + lax.ppermute(send, "xh", swap).astype(f32)
    k_new = base + (step_size * samp_weight) * k_sum
    return (k_new.reshape(basis_u.shape), l_new)


def solution(mesh):
    fine = Mesh(mesh.devices.reshape(4, 2, 2, 4, 2), SPACE + SAMP)
    return jax.shard_map(
        per_device,
        mesh=fine,
        in_specs=(P(SAMP, SPACE, None, None), P(SPACE, SAMP), P(), P(None, SPACE, None, None), P(SAMP)),
        out_specs=(P(SAMP, SPACE, None, None), P(SPACE, SAMP)),
        check_vma=False,
    )
```

```python
import functools

import jax
import jax.numpy as jnp
from jax import lax
from jax.experimental import pallas as pl
from jax.experimental.pallas import tpu as pltpu
from jax.sharding import Mesh, PartitionSpec as P

step_size = 0.1
SPACE = ("z", "xl", "c")
SAMP = ("y", "xh")
BLOCK = 2048
bf16, f32 = jnp.bfloat16, jnp.float32


def dot(a, b, ca, cb):
    return lax.dot_general(a, b, (((ca,), (cb,)), ((), ())), preferred_element_type=f32)


def resident(x):
    return pltpu.with_memory_space_constraint(x, pltpu.MemorySpace.VMEM)


def small(body, args, outs, scratch=(), at=None, held=(), limit=24):
    vm = pl.BlockSpec(memory_space=pltpu.VMEM)
    scalars = [] if at is None else [at]
    n_read = len(scalars) + len(args)

    def reading(*refs):
        body(*refs[:n_read], *refs[n_read + len(held) :])

    return pl.pallas_call(
        reading,
        in_specs=[pl.BlockSpec(memory_space=pltpu.SMEM)] * len(scalars)
        + [vm] * (len(args) + len(held)),
        out_specs=[vm] * len(outs),
        out_shape=[(pltpu.VMEM if keep else pltpu.HBM)(shape, dtype) for shape, dtype, keep in outs],
        scratch_shapes=[pltpu.VMEM(shape, dtype) for shape, dtype in scratch],
        compiler_params=pltpu.CompilerParams(vmem_limit_bytes=limit << 20),
    )(*scalars, *args, *held)


def head_body(u_ref, v_ref, flat_ref, out_ref, u_s):
    _, depth, rows, cols = u_ref.shape
    u_s[...] = u_ref[...].astype(f32)
    for x in range(depth):
        for y in range(rows):
            at = (x * rows + y) * cols
            flat_ref[:, at : at + cols] = u_s[:, x, y, :].astype(bf16)
    half = out_ref.shape[-1]
    for k in range(out_ref.shape[0]):
        out_ref[k, 0] = v_ref[:, :half]
        out_ref[k, 1] = v_ref[:, half:]


def prep_body(at_ref, u_ref, w_ref, a_ref, b_ref, c_ref, core_ref, full_ref, k_ref, kt_ref, halo_ref):
    narrow, cells = u_ref.shape
    half = cells // 2
    y, xh = at_ref[2], at_ref[3]

    def put(turn, flip, value):
        row = (((y + turn) % 4) * 2 + (xh if flip == 0 else 1 - xh)) * narrow
        full_ref[pl.ds(pl.multiple_of(row, narrow), narrow), :] = value

    put(0, 0, u_ref[...])
    put(0, 1, w_ref[...])
    for turn, ref in ((3, a_ref), (1, b_ref), (2, c_ref)):
        put(turn, 0, ref[:narrow, :])
        put(turn, 1, ref[narrow:, :])
    k_own = dot(core_ref[...].astype(bf16), full_ref[...], 0, 0).astype(bf16)
    k_ref[...] = k_own
    kt_ref[...] = k_own.T
    first = at_ref[0] == 0

    @pl.when(first)
    def _():
        halo_ref[...] = k_own[:, :half]

    @pl.when(jnp.logical_not(first))
    def _():
        halo_ref[...] = k_own[:, half:]


def mid_body(rows, cols, c_ref, oth_ref, core_ref, k_ref, halo_ref, face_ref, u_ref, kt_ref, base_ref, m_ref, base_s, lap_s):
    half = oth_ref.shape[1] // 2
    k_oth = dot(core_ref[...].astype(bf16), oth_ref[...], 0, 0).astype(bf16)
    kt_ref[...] = k_oth.T
    first = c_ref[0] == 0
    near = jnp.where(first, k_oth[:, :half].astype(f32), k_oth[:, half:].astype(f32))
    halo = halo_ref[...].astype(f32)
    before = jnp.where(first, halo, near)
    after = jnp.where(first, near, halo)
    plane = rows * cols
    lane = lax.broadcasted_iota(jnp.int32, (1, cols), 1)
    for x in range(2):
        for y in range(rows):
            at = (x * rows + y) * cols
            mid = k_ref[:, at : at + cols].astype(f32)
            w = [0.25 * lax.shift_left(1, face_ref[f, x, y : y + 1, :]).astype(f32) for f in range(6)]
            total = ((w[0] + w[1]) + (w[2] + w[3])) + (w[4] + w[5])
            down = before[:, y * cols : (y + 1) * cols] if x == 0 else k_ref[:, at - plane : at - plane + cols].astype(f32)
            up = after[:, y * cols : (y + 1) * cols] if x == 1 else k_ref[:, at + plane : at + plane + cols].astype(f32)
            out = w[0] * down + w[1] * up - total * mid
            if y > 0:
                out += w[2] * k_ref[:, at - cols : at].astype(f32)
            if y < rows - 1:
                out += w[3] * k_ref[:, at + cols : at + 2 * cols].astype(f32)
            out += jnp.where(lane == 0, 0.0, w[4]) * pltpu.roll(mid, 1, 1)
            out += jnp.where(lane == cols - 1, 0.0, w[5]) * pltpu.roll(mid, cols - 1, 1)
            base_s[:, at : at + cols] = mid + step_size * out
            lap_s[:, at : at + cols] = out.astype(bf16)
    base_ref[...] = base_s[pl.ds(pl.multiple_of(c_ref[1] * base_ref.shape[0], 8), base_ref.shape[0]), :]
    m_ref[...] = dot(u_ref[...], lap_s[...], 1, 1)


def sweep(kt_ref, u_ref, v_ref, g_ref, ov_ref, start, stop, store, tile=512):
    block = min(BLOCK, stop - start)

    def turn(i, _):
        at = pl.multiple_of(start + i * block, block)
        v = v_ref[:, pl.ds(at, block)]
        g = g_ref[:, pl.ds(at, block)]
        acc = None
        for row in range(0, u_ref.shape[1], tile):
            field = dot(kt_ref[row : row + tile, :], v, 1, 0)
            react = (field * (g - field * field)).astype(bf16)
            ov_ref[row : row + tile, :] += dot(react, v, 1, 1)
            part = dot(u_ref[:, row : row + tile], react, 1, 0)
            acc = part if acc is None else acc + part
        store(pl.ds(pl.multiple_of(at - start, block), block), acc)
        return 0

    lax.fori_loop(0, (stop - start) // block, turn, 0)


def part_body(start, has_old, back, kt_ref, u_ref, v_ref, g_ref, *refs):
    refs = list(refs)
    old_ref = refs.pop(0) if has_old & 1 else None
    far_ref = refs.pop(0) if has_old & 2 else None
    l_ref, ov_ref = refs[:2]
    ov_s = refs[2] if back else ov_ref
    ov_s[...] = jnp.zeros_like(ov_s) if far_ref is None else far_ref[...]

    def store(here, acc):
        l_ref[:, here] = acc if old_ref is None else old_ref[:, here] + acc

    stop = start + l_ref.shape[1]
    done = 0 if old_ref is None else old_ref.shape[1]
    if done:
        sweep(kt_ref, u_ref, v_ref, g_ref, ov_s, start, start + done, store)
    if start + done < stop:

        def rest(here, acc):
            l_ref[:, pl.ds(pl.multiple_of(here.start + done, done or BLOCK), here.size)] = acc

        sweep(kt_ref, u_ref, v_ref, g_ref, ov_s, start + done, stop, rest)
    if back:
        ov_ref[...] = ov_s[...].T.astype(bf16)


def last_body(
    scale, at_ref, kt_ref, u_ref, v_ref, g_ref, l_ref, more_ref, ov_ref, got_ref, ma_ref, mb_ref, core_ref,
    out_ref, me_ref, up_ref, dn_ref, away_ref, ov_s, tot_s, w_s,
):
    rank, count = out_ref.shape
    middle = count - count // 2
    start = middle + more_ref.shape[1]
    ov_s[...] = ov_ref[...]
    w = core_ref[...].astype(bf16).astype(f32) * 0.125 + scale * (ma_ref[...] + mb_ref[...])
    high = w.astype(bf16)
    w_s[:rank, :] = high
    w_s[rank:, :] = (w - high.astype(f32)).astype(bf16)

    def send(at, size, total):
        side = dot(w_s[...], v_ref[:, at : at + size], 1, 0)
        out_ref[:, at : at + size] = (scale * total + (side[:rank] + side[rank:])).astype(bf16)

    send(0, middle, l_ref[:, :middle])
    send(middle, start - middle, l_ref[:, middle:start] + more_ref[...])

    def store(here, acc):
        send(start, count - start, l_ref[:, start:] + acc)

    sweep(kt_ref, u_ref, v_ref, g_ref, ov_s, start, count, store)
    tot_s[...] = ov_s[...].T + got_ref[...].astype(f32)
    rows = me_ref.shape[0]
    y = at_ref[2]

    def part(turn):
        return tot_s[pl.ds(pl.multiple_of(((y + turn) % 4) * rows, rows), rows), :]

    me_ref[...] = part(0)
    up_ref[...] = part(1).astype(bf16)
    away_ref[...] = part(2).astype(bf16)
    dn_ref[...] = part(3).astype(bf16)


def done_body(scale, base_ref, mine_ref, got_ref, out_ref):
    _, depth, rows, cols = out_ref.shape
    new = base_ref[...] + scale * (mine_ref[...] + got_ref[...].astype(f32))
    for x in range(depth):
        for y in range(rows):
            at = (x * rows + y) * cols
            out_ref[:, x, y, :] = new[:, at : at + cols]


def pair_body(at_ref, me_ref, rc_ref, rd_ref, re_ref, mine_ref, send_ref, tot_s):
    rows = mine_ref.shape[0]
    tot_s[...] = (me_ref[...] + rc_ref[...].astype(f32)) + (rd_ref[...].astype(f32) + re_ref[...].astype(f32))
    xh = at_ref[3]
    mine_ref[...] = tot_s[pl.ds(pl.multiple_of(xh * rows, rows), rows), :]
    send_ref[...] = tot_s[pl.ds(pl.multiple_of((1 - xh) * rows, rows), rows), :].astype(bf16)


def ring(n, k):
    return [(i, (i + k) % n) for i in range(n)]


def per_device(basis_u, basis_v, core_s, face_class, sample_class):
    narrow, depth_x, rows_y, cols_z = basis_u.shape
    rank = core_s.shape[0]
    n_samp, n_space = 8, 16
    cells = depth_x * rows_y * cols_z
    lanes, samp_rows = basis_v.shape
    half = samp_rows // 2
    cell_weight = rank / (cells * n_space)
    samp_weight = rank / (samp_rows * n_samp)
    core_at = lax.axis_index("c")
    where_at = jnp.stack([core_at, lax.axis_index(SAMP), lax.axis_index("y"), lax.axis_index("xh")]).astype(jnp.int32)
    swap = ring(2, 1)

    u0, v_wide = small(
        head_body,
        [basis_u, basis_v],
        [((narrow, cells), bf16, True), ((n_space // 2, 2, lanes, half), bf16, False)],
        [(basis_u.shape, f32)],
    )
    v = resident(lax.all_to_all(v_wide.reshape(rank, half), SPACE, 0, 0, tiled=True))
    u1 = lax.ppermute(u0, "xh", swap)
    pair = jnp.concatenate([u0, u1], 0)
    around = [resident(lax.ppermute(pair, "y", ring(4, k))) for k in (1, 3, 2)]
    u_own, k_own, kt_own, edge = small(
        prep_body,
        [u0, resident(u1), *around, core_s],
        [((rank, cells), bf16, True), ((rank, cells), bf16, True), ((cells, rank), bf16, True), ((rank, cells // 2), bf16, True)],
        at=where_at,
    )
    u_oth = resident(lax.ppermute(u_own, "c", swap))
    chips = n_space // 2
    hops = [(2 * i + 1, 2 * i + 2) for i in range(chips - 1)] + [(2 * i + 2, 2 * i + 1) for i in range(chips - 1)]
    halo = resident(lax.ppermute(edge, SPACE, hops))

    growth = 0.5 + 0.5 * lax.dynamic_slice_in_dim(sample_class, core_at * half, half, 0).astype(f32)
    growth = resident(growth.reshape(1, half))
    scale = step_size * cell_weight
    quart = half // 2
    main = lambda start, kinds, back: functools.partial(part_body, start, kinds, back)
    l_first, ov_first = small(
        main(0, 0, False), [kt_own, u_own, v, growth], [((rank, quart), f32, True), ((cells, rank), f32, True)]
    )
    kt_oth, base, m_own = small(
        functools.partial(mid_body, rows_y, cols_z),
        [u_oth, core_s, k_own, halo, face_class, u_own],
        [((cells, rank), bf16, True), ((narrow, cells), f32, False), ((rank, rank), f32, True)],
        [((rank, cells), f32), ((rank, cells), bf16)],
        at=where_at,
        held=(ov_first, kt_own, l_first),
    )
    m_oth = resident(lax.ppermute(m_own, "c", swap))
    l_most, ov_send = small(
        main(0, 1, True),
        [kt_oth, u_oth, v, growth, l_first],
        [((rank, half), f32, True), ((rank, cells), bf16, True)],
        [((cells, rank), f32)],
        held=(ov_first, kt_own, u_own),
    )
    got = resident(lax.ppermute(ov_send, "c", swap))
    l_more, ov_more = small(
        main(quart, 2, False),
        [kt_own, u_own, v, growth, ov_first],
        [((rank, quart // 2), f32, True), ((cells, rank), f32, True)],
        held=(l_most, ov_send),
    )
    rows = rank // 4
    l_part, me, up, dn, away = small(
        functools.partial(last_body, scale),
        [kt_own, u_own, v, growth, l_most, l_more, ov_more, got, m_own, m_oth, core_s],
        [((rank, half), bf16, False), ((rows, cells), f32, True)] + [((rows, cells), bf16, True)] * 3,
        [((cells, rank), f32), ((rank, cells), f32), ((2 * rank, rank), bf16)],
        at=where_at,
    )

    l_got = lax.all_to_all(l_part, SPACE, 0, 0, tiled=True)
    l_new = l_got.reshape(n_space // 2, 2, lanes, half).astype(f32).sum(0)
    l_new = jnp.transpose(l_new, (1, 0, 2)).reshape(lanes, samp_rows)

    near = [resident(lax.ppermute(part, "y", ring(4, k))) for part, k in ((up, 1), (dn, 3), (away, 2))]
    mine, send = small(
        pair_body,
        [me, *near],
        [((narrow, cells), f32, True), ((narrow, cells), bf16, True)],
        [((rows, cells), f32)],
        at=where_at,
    )
    (k_new,) = small(
        functools.partial(done_body, step_size * samp_weight),
        [base, mine, resident(lax.ppermute(send, "xh", swap))],
        [(basis_u.shape, f32, False)],
    )
    return (k_new, l_new)


def solution(mesh):
    fine = Mesh(mesh.devices.reshape(4, 2, 2, 4, 2), SPACE + SAMP)
    return jax.shard_map(
        per_device,
        mesh=fine,
        in_specs=(P(SAMP, SPACE, None, None), P(SPACE, SAMP), P(), P(None, SPACE, None, None), P(SAMP)),
        out_specs=(P(SAMP, SPACE, None, None), P(SPACE, SAMP)),
        check_vma=False,
    )
```

```python
import functools

import jax
import jax.numpy as jnp
from jax import lax
from jax.experimental import pallas as pl
from jax.experimental.pallas import tpu as pltpu
from jax.sharding import Mesh, PartitionSpec as P

step_size = 0.1
SPACE = ("z", "xl", "c")
SAMP = ("y", "xh")
BLOCK = 2048
bf16, f32 = jnp.bfloat16, jnp.float32


def dot(a, b, ca, cb):
    return lax.dot_general(a, b, (((ca,), (cb,)), ((), ())), preferred_element_type=f32)


def resident(x):
    return pltpu.with_memory_space_constraint(x, pltpu.MemorySpace.VMEM)


def small(body, args, outs, scratch=(), at=None, held=(), limit=24):
    vm = pl.BlockSpec(memory_space=pltpu.VMEM)
    scalars = [] if at is None else [at]
    n_read = len(scalars) + len(args)

    def reading(*refs):
        body(*refs[:n_read], *refs[n_read + len(held) :])

    return pl.pallas_call(
        reading,
        in_specs=[pl.BlockSpec(memory_space=pltpu.SMEM)] * len(scalars)
        + [vm] * (len(args) + len(held)),
        out_specs=[vm] * len(outs),
        out_shape=[(pltpu.VMEM if keep else pltpu.HBM)(shape, dtype) for shape, dtype, keep in outs],
        scratch_shapes=[pltpu.VMEM(shape, dtype) for shape, dtype in scratch],
        compiler_params=pltpu.CompilerParams(vmem_limit_bytes=limit << 20),
    )(*scalars, *args, *held)


def head_body(at_ref, u_hbm, v_hbm, flat_ref, keep_ref, send_ref, u_s, w_s, v_s, sems):
    fetch = [pltpu.make_async_copy(v_hbm, v_s, sems.at[0]), pltpu.make_async_copy(u_hbm, u_s, sems.at[1])]
    for copy in fetch:
        copy.start()
    half = keep_ref.shape[1]
    first = at_ref[0] == 0
    fetch[0].wait()

    @pl.when(first)
    def _():
        keep_ref[...] = v_s[:, :half]
        send_ref[...] = v_s[:, half:]

    @pl.when(jnp.logical_not(first))
    def _():
        keep_ref[...] = v_s[:, half:]
        send_ref[...] = v_s[:, :half]

    fetch[1].wait()
    _, depth, rows, cols = u_s.shape
    w_s[...] = u_s[...].astype(f32)
    for x in range(depth):
        for y in range(rows):
            at = (x * rows + y) * cols
            flat_ref[:, at : at + cols] = w_s[:, x, y, :].astype(bf16)


def stack_body(which, at_ref, mine_ref, got_ref, *outs):
    rows = mine_ref.shape[0]
    width = outs[0].shape[1]

    def put(top_ref, low_ref):
        for i, out_ref in enumerate(outs):
            out_ref[:rows, :] = top_ref[:, i * width : (i + 1) * width]
            out_ref[rows:, :] = low_ref[:, i * width : (i + 1) * width]

    first = at_ref[which] == 0

    @pl.when(first)
    def _():
        put(mine_ref, got_ref)

    @pl.when(jnp.logical_not(first))
    def _():
        put(got_ref, mine_ref)


def gather_rows(z, pieces, v_ref):
    rows = pieces[0].shape[0]
    for turn, piece in zip((0, 3, 1, 2), pieces):
        v_ref[pl.ds(pl.multiple_of(((z + turn) % 4) * rows, rows), rows), :] = piece[...]


def prep_body(at_ref, p0, p1, p2, p3, core_ref, full_ref, k_ref, kt_ref, halo_ref):
    half = full_ref.shape[1] // 2
    gather_rows(at_ref[2], (p0, p1, p2, p3), full_ref)
    k_own = dot(core_ref[...].astype(bf16), full_ref[...], 0, 0).astype(bf16)
    k_ref[...] = k_own
    kt_ref[...] = k_own.T
    first = at_ref[0] == 0

    @pl.when(first)
    def _():
        halo_ref[...] = k_own[:, :half]

    @pl.when(jnp.logical_not(first))
    def _():
        halo_ref[...] = k_own[:, half:]


def mid_body(rows, cols, c_ref, oth_ref, core_ref, k_ref, halo_ref, face_ref, u_ref, kt_ref, base_ref, m_ref, base_s, lap_s):
    half = oth_ref.shape[1] // 2
    k_oth = dot(core_ref[...].astype(bf16), oth_ref[...], 0, 0).astype(bf16)
    kt_ref[...] = k_oth.T
    first = c_ref[0] == 0
    near = jnp.where(first, k_oth[:, :half].astype(f32), k_oth[:, half:].astype(f32))
    halo = halo_ref[...].astype(f32)
    before = jnp.where(first, halo, near)
    after = jnp.where(first, near, halo)
    plane = rows * cols
    lane = lax.broadcasted_iota(jnp.int32, (1, cols), 1)
    for x in range(2):
        for y in range(rows):
            at = (x * rows + y) * cols
            mid = k_ref[:, at : at + cols].astype(f32)
            w = [0.25 * lax.shift_left(1, face_ref[f, x, y : y + 1, :]).astype(f32) for f in range(6)]
            total = ((w[0] + w[1]) + (w[2] + w[3])) + (w[4] + w[5])
            down = before[:, y * cols : (y + 1) * cols] if x == 0 else k_ref[:, at - plane : at - plane + cols].astype(f32)
            up = after[:, y * cols : (y + 1) * cols] if x == 1 else k_ref[:, at + plane : at + plane + cols].astype(f32)
            out = w[0] * down + w[1] * up - total * mid
            if y > 0:
                out += w[2] * k_ref[:, at - cols : at].astype(f32)
            if y < rows - 1:
                out += w[3] * k_ref[:, at + cols : at + 2 * cols].astype(f32)
            out += jnp.where(lane == 0, 0.0, w[4]) * pltpu.roll(mid, 1, 1)
            out += jnp.where(lane == cols - 1, 0.0, w[5]) * pltpu.roll(mid, cols - 1, 1)
            base_s[:, at : at + cols] = mid + step_size * out
            lap_s[:, at : at + cols] = out.astype(bf16)
    base_ref[...] = base_s[pl.ds(pl.multiple_of(c_ref[1] * base_ref.shape[0], 8), base_ref.shape[0]), :]
    m_ref[...] = dot(u_ref[...], lap_s[...], 1, 1)


def sweep(kt_ref, u_ref, v_ref, g_ref, ov_ref, store, start=0, stop=None, tile=512):
    stop = v_ref.shape[1] if stop is None else stop
    block = min(BLOCK, stop - start)
    for at in range(start, stop, block):
        v = v_ref[:, at : at + block]
        g = g_ref[:, at : at + block]
        acc = None
        for row in range(0, u_ref.shape[1], tile):
            field = dot(kt_ref[row : row + tile, :], v, 1, 0)
            react = (field * (g - field * field)).astype(bf16)
            ov_ref[row : row + tile, :] += dot(react, v, 1, 1)
            part = dot(u_ref[:, row : row + tile], react, 1, 0)
            acc = part if acc is None else acc + part
        store(at, block, acc)


def own_body(at_ref, kt_ref, u_ref, g_ref, p0, p1, p2, p3, l_ref, ov_ref, v_ref):
    gather_rows(at_ref[4], (p0, p1, p2, p3), v_ref)
    ov_ref[...] = jnp.zeros_like(ov_ref)

    def store(at, size, acc):
        l_ref[:, at : at + size] = acc

    sweep(kt_ref, u_ref, v_ref, g_ref, ov_ref, store)


def oth_body(at_ref, kt_ref, u_ref, g0_ref, g1_ref, v0_ref, old_ref, p0, p1, p2, p3, l0_ref, l1_ref, send_ref, v1_ref, ov_s):
    gather_rows(at_ref[4], (p0, p1, p2, p3), v1_ref)
    ov_s[...] = jnp.zeros_like(ov_s)

    def store0(at, size, acc):
        l0_ref[:, at : at + size] = old_ref[:, at : at + size] + acc

    def store1(at, size, acc):
        l1_ref[:, at : at + size] = acc

    sweep(kt_ref, u_ref, v0_ref, g0_ref, ov_s, store0)
    sweep(kt_ref, u_ref, v1_ref, g1_ref, ov_s, store1)
    send_ref[...] = ov_s[...].T.astype(bf16)


def last_body(
    scale, kt_ref, u_ref, g_ref, v0_ref, v1_ref, l0_ref, l1_ref, ov_old_ref, ma_ref, mb_ref, core_ref, out_ref, ov_ref, w_s
):
    rank = out_ref.shape[0]
    half = v0_ref.shape[1]
    ov_ref[...] = ov_old_ref[...]
    w = core_ref[...].astype(bf16).astype(f32) * 0.125 + scale * (ma_ref[...] + mb_ref[...])
    high = w.astype(bf16)
    w_s[:rank, :] = high
    w_s[rank:, :] = (w - high.astype(f32)).astype(bf16)

    def send(v, at, total):
        side = dot(w_s[...], v, 1, 0)
        out_ref[:, at : at + total.shape[1]] = (scale * total + (side[:rank] + side[rank:])).astype(bf16)

    send(v0_ref[...], 0, l0_ref[...])

    def store(at, size, acc):
        send(v1_ref[:, at : at + size], half + at, l1_ref[:, at : at + size] + acc)

    sweep(kt_ref, u_ref, v1_ref, g_ref, ov_ref, store)


def turn_body(at_ref, ov_ref, got_ref, me_ref, *refs):
    outs, tot_s = refs[:-1], refs[-1]
    tot_s[...] = ov_ref[...].T + got_ref[...].astype(f32)
    rows = me_ref.shape[0]
    n_samp = tot_s.shape[0] // rows

    def part(turn):
        return tot_s[pl.ds(pl.multiple_of(((at_ref[1] + turn) % n_samp) * rows, rows), rows), :]

    me_ref[...] = part(0)
    for turn, out_ref in enumerate(outs, 1):
        out_ref[...] = part(turn).astype(bf16)


def done_body(scale, base_ref, mine_ref, *refs):
    parts, out_ref = refs[:-1], refs[-1]
    _, depth, rows, cols = out_ref.shape
    total = mine_ref[...]
    for part in parts:
        total = total + part[...].astype(f32)
    new = base_ref[...] + scale * total
    for x in range(depth):
        for y in range(rows):
            at = (x * rows + y) * cols
            out_ref[:, x, y, :] = new[:, at : at + cols]


def send(x, axis, hops):
    return resident(lax.ppermute(x, axis, hops))


def ring(n, k):
    return [(i, (i + k) % n) for i in range(n)]


def per_device(basis_u, basis_v, core_s, face_class, sample_class):
    narrow, depth_x, rows_y, cols_z = basis_u.shape
    rank = core_s.shape[0]
    n_samp, n_space = 8, 16
    cells = depth_x * rows_y * cols_z
    lanes, samp_rows = basis_v.shape
    half = samp_rows // 2
    cell_weight = rank / (cells * n_space)
    samp_weight = rank / (samp_rows * n_samp)
    core_at = lax.axis_index("c")
    places = (core_at, lax.axis_index(SAMP)) + tuple(lax.axis_index(n) for n in ("y", "xh", "z", "xl"))
    where_at = jnp.stack(places).astype(jnp.int32)
    swap = ring(2, 1)

    quart = half // 2
    far = pl.BlockSpec(memory_space=pltpu.MemorySpace.HBM)
    vmem = pl.BlockSpec(memory_space=pltpu.VMEM)
    u0, v_keep, v_send = pl.pallas_call(
        head_body,
        in_specs=[pl.BlockSpec(memory_space=pltpu.SMEM), far, far],
        out_specs=[vmem] * 3,
        out_shape=[pltpu.VMEM((narrow, cells), bf16)] + [pltpu.VMEM((lanes, half), bf16)] * 2,
        scratch_shapes=[
            pltpu.VMEM(basis_u.shape, bf16),
            pltpu.VMEM(basis_u.shape, f32),
            pltpu.VMEM(basis_v.shape, bf16),
            pltpu.SemaphoreType.DMA((2,)),
        ],
        compiler_params=pltpu.CompilerParams(vmem_limit_bytes=24 << 20),
    )(where_at, basis_u, basis_v)
    u1 = send(u0, "xh", swap)
    v_got = send(v_send, "c", swap)
    (v_chip,) = small(functools.partial(stack_body, 0), [v_keep, v_got], [((2 * lanes, half), bf16, True)], at=where_at)
    v_next = send(v_chip, "xl", swap)
    v_mine = small(functools.partial(stack_body, 5), [v_chip, v_next], [((4 * lanes, quart), bf16, True)] * 2, at=where_at)
    v_pieces = [[m] + [send(m, "z", ring(4, k)) for k in (1, 3, 2)] for m in v_mine]
    (pair,) = small(functools.partial(stack_body, 3), [u0, u1], [((2 * narrow, cells), bf16, True)], at=where_at)
    around = [send(pair, "y", ring(4, k)) for k in (1, 3, 2)]
    u_own, k_own, kt_own, edge = small(
        prep_body,
        [pair, *around, core_s],
        [((rank, cells), bf16, True), ((rank, cells), bf16, True), ((cells, rank), bf16, True), ((rank, cells // 2), bf16, True)],
        at=where_at,
    )
    u_oth = send(u_own, "c", swap)
    chips = n_space // 2
    hops = [(2 * i + 1, 2 * i + 2) for i in range(chips - 1)] + [(2 * i + 2, 2 * i + 1) for i in range(chips - 1)]
    halo = send(edge, SPACE, hops)

    growth = 0.5 + 0.5 * lax.dynamic_slice_in_dim(sample_class, core_at * half, half, 0).astype(f32)
    growth = [resident(growth[i * quart : (i + 1) * quart].reshape(1, quart)) for i in range(2)]
    scale = step_size * cell_weight
    l_first, ov_first, v0 = small(
        own_body,
        [kt_own, u_own, growth[0], *v_pieces[0]],
        [((rank, quart), f32, True), ((cells, rank), f32, True), ((rank, quart), bf16, True)],
        at=where_at,
    )
    kt_oth, base, m_own = small(
        functools.partial(mid_body, rows_y, cols_z),
        [u_oth, core_s, k_own, halo, face_class, u_own],
        [((cells, rank), bf16, True), ((narrow, cells), f32, False), ((rank, rank), f32, True)],
        [((rank, cells), f32), ((rank, cells), bf16)],
        at=where_at,
        held=(ov_first, kt_own, l_first),
    )
    m_oth = send(m_own, "c", swap)
    l0, l1, ov_send, v1 = small(
        oth_body,
        [kt_oth, u_oth, *growth, v0, l_first, *v_pieces[1]],
        [((rank, quart), f32, True), ((rank, quart), f32, True), ((rank, cells), bf16, True), ((rank, quart), bf16, True)],
        [((cells, rank), f32)],
        at=where_at,
        held=(ov_first, kt_own, u_own),
    )
    got = send(ov_send, "c", swap)
    l_part, ov_own = small(
        functools.partial(last_body, scale),
        [kt_own, u_own, growth[1], v0, v1, l0, l1, ov_first, m_own, m_oth, core_s],
        [((rank, half), bf16, False), ((cells, rank), f32, True)],
        [((2 * rank, rank), bf16)],
    )

    l_got = lax.all_to_all(l_part, SPACE, 0, 0, tiled=True)
    l_new = l_got.reshape(n_space // 2, 2, lanes, half).astype(f32).sum(0)
    l_new = jnp.transpose(l_new, (1, 0, 2)).reshape(lanes, samp_rows)

    me, *others = small(
        turn_body,
        [ov_own, got],
        [((narrow, cells), f32, True)] + [((narrow, cells), bf16, True)] * (n_samp - 1),
        [((rank, cells), f32)],
        at=where_at,
    )
    sums = [send(part, SAMP, ring(n_samp, turn)) for turn, part in enumerate(others, 1)]
    (k_new,) = small(
        functools.partial(done_body, step_size * samp_weight), [base, me, *sums], [(basis_u.shape, f32, False)]
    )
    return (k_new, l_new)


def solution(mesh):
    fine = Mesh(mesh.devices.reshape(4, 2, 2, 4, 2), SPACE + SAMP)
    return jax.shard_map(
        per_device,
        mesh=fine,
        in_specs=(P(SAMP, SPACE, None, None), P(SPACE, SAMP), P(), P(None, SPACE, None, None), P(SAMP)),
        out_specs=(P(SAMP, SPACE, None, None), P(SPACE, SAMP)),
        check_vma=False,
    )
```

```python
import functools

import jax
import jax.numpy as jnp
from jax import lax
from jax.experimental import pallas as pl
from jax.experimental.pallas import tpu as pltpu
from jax.sharding import Mesh, PartitionSpec as P

step_size = 0.1
SPACE = ("z", "xl", "c")
SAMP = ("y", "xh")
BLOCK = 2048
bf16, f32 = jnp.bfloat16, jnp.float32


def dot(a, b, ca, cb):
    return lax.dot_general(a, b, (((ca,), (cb,)), ((), ())), preferred_element_type=f32)


def resident(x):
    return pltpu.with_memory_space_constraint(x, pltpu.MemorySpace.VMEM)


def small(body, args, outs, scratch=(), at=None, held=(), limit=24):
    vm = pl.BlockSpec(memory_space=pltpu.VMEM)
    scalars = [] if at is None else [at]
    n_read = len(scalars) + len(args)

    def reading(*refs):
        body(*refs[:n_read], *refs[n_read + len(held) :])

    return pl.pallas_call(
        reading,
        in_specs=[pl.BlockSpec(memory_space=pltpu.SMEM)] * len(scalars)
        + [vm] * (len(args) + len(held)),
        out_specs=[vm] * len(outs),
        out_shape=[(pltpu.VMEM if keep else pltpu.HBM)(shape, dtype) for shape, dtype, keep in outs],
        scratch_shapes=[pltpu.VMEM(shape, dtype) for shape, dtype in scratch],
        compiler_params=pltpu.CompilerParams(vmem_limit_bytes=limit << 20),
    )(*scalars, *args, *held)


def stack_body(which, at_ref, mine_ref, got_ref, *outs):
    rows = mine_ref.shape[0]
    width = outs[0].shape[1]

    def put(top_ref, low_ref):
        for i, out_ref in enumerate(outs):
            out_ref[:rows, :] = top_ref[:, i * width : (i + 1) * width]
            out_ref[rows:, :] = low_ref[:, i * width : (i + 1) * width]

    first = at_ref[which] == 0

    @pl.when(first)
    def _():
        put(mine_ref, got_ref)

    @pl.when(jnp.logical_not(first))
    def _():
        put(got_ref, mine_ref)


def gather_rows(z, pieces, v_ref):
    rows = pieces[0].shape[0]
    for turn, piece in zip((0, 3, 1, 2), pieces):
        v_ref[pl.ds(pl.multiple_of(((z + turn) % 4) * rows, rows), rows), :] = piece[...]


def prep_body(at_ref, p0, p1, p2, p3, core_ref, full_ref, k_ref, kt_ref, halo_ref):
    half = full_ref.shape[1] // 2
    gather_rows(at_ref[2], (p0, p1, p2, p3), full_ref)
    k_own = dot(core_ref[...].astype(bf16), full_ref[...], 0, 0).astype(bf16)
    k_ref[...] = k_own
    kt_ref[...] = k_own.T
    first = at_ref[0] == 0

    @pl.when(first)
    def _():
        halo_ref[...] = k_own[:, :half]

    @pl.when(jnp.logical_not(first))
    def _():
        halo_ref[...] = k_own[:, half:]


def mid_body(rows, cols, c_ref, oth_ref, core_ref, k_ref, halo_ref, face_ref, u_ref, kt_ref, base_ref, m_ref, base_s, lap_s):
    half = oth_ref.shape[1] // 2
    k_oth = dot(core_ref[...].astype(bf16), oth_ref[...], 0, 0).astype(bf16)
    kt_ref[...] = k_oth.T
    first = c_ref[0] == 0
    near = jnp.where(first, k_oth[:, :half].astype(f32), k_oth[:, half:].astype(f32))
    halo = halo_ref[...].astype(f32)
    before = jnp.where(first, halo, near)
    after = jnp.where(first, near, halo)
    plane = rows * cols
    lane = lax.broadcasted_iota(jnp.int32, (1, cols), 1)
    for x in range(2):
        for y in range(rows):
            at = (x * rows + y) * cols
            mid = k_ref[:, at : at + cols].astype(f32)
            w = [0.25 * lax.shift_left(1, face_ref[f, x, y : y + 1, :]).astype(f32) for f in range(6)]
            total = ((w[0] + w[1]) + (w[2] + w[3])) + (w[4] + w[5])
            down = before[:, y * cols : (y + 1) * cols] if x == 0 else k_ref[:, at - plane : at - plane + cols].astype(f32)
            up = after[:, y * cols : (y + 1) * cols] if x == 1 else k_ref[:, at + plane : at + plane + cols].astype(f32)
            out = w[0] * down + w[1] * up - total * mid
            if y > 0:
                out += w[2] * k_ref[:, at - cols : at].astype(f32)
            if y < rows - 1:
                out += w[3] * k_ref[:, at + cols : at + 2 * cols].astype(f32)
            out += jnp.where(lane == 0, 0.0, w[4]) * pltpu.roll(mid, 1, 1)
            out += jnp.where(lane == cols - 1, 0.0, w[5]) * pltpu.roll(mid, cols - 1, 1)
            base_s[:, at : at + cols] = mid + step_size * out
            lap_s[:, at : at + cols] = out.astype(bf16)
    base_ref[...] = base_s[pl.ds(pl.multiple_of(c_ref[1] * base_ref.shape[0], 8), base_ref.shape[0]), :]
    m_ref[...] = dot(u_ref[...], lap_s[...], 1, 1)


def sweep(kt_ref, u_ref, v_ref, g_ref, ov_ref, store, start=0, stop=None, tile=512):
    stop = v_ref.shape[1] if stop is None else stop
    block = min(BLOCK, stop - start)
    for at in range(start, stop, block):
        v = v_ref[:, at : at + block]
        g = g_ref[:, at : at + block]
        acc = None
        for row in range(0, u_ref.shape[1], tile):
            field = dot(kt_ref[row : row + tile, :], v, 1, 0)
            react = (field * (g - field * field)).astype(bf16)
            ov_ref[row : row + tile, :] += dot(react, v, 1, 1)
            part = dot(u_ref[:, row : row + tile], react, 1, 0)
            acc = part if acc is None else acc + part
        store(at, block, acc)


def own_body(kt_ref, u_ref, v_ref, g_ref, l_ref, ov_ref):
    ov_ref[...] = jnp.zeros_like(ov_ref)

    def store(at, size, acc):
        l_ref[:, at : at + size] = acc

    sweep(kt_ref, u_ref, v_ref, g_ref, ov_ref, store, 0, l_ref.shape[1])


def oth_body(kt_ref, u_ref, v_ref, g_ref, old_ref, l_ref, send_ref, ov_s):
    ov_s[...] = jnp.zeros_like(ov_s)
    done = old_ref.shape[1]

    def store(at, size, acc):
        l_ref[:, at : at + size] = acc + old_ref[:, at : at + size] if at < done else acc

    sweep(kt_ref, u_ref, v_ref, g_ref, ov_s, store)
    send_ref[...] = ov_s[...].T.astype(bf16)


def last_body(scale, kt_ref, u_ref, v_ref, g_ref, l_ref, ov_old_ref, ma_ref, mb_ref, core_ref, out_ref, ov_ref, w_s):
    rank, count = out_ref.shape
    ov_ref[...] = ov_old_ref[...]
    w = core_ref[...].astype(bf16).astype(f32) * 0.125 + scale * (ma_ref[...] + mb_ref[...])
    high = w.astype(bf16)
    w_s[:rank, :] = high
    w_s[rank:, :] = (w - high.astype(f32)).astype(bf16)

    def send_on(at, size, acc):
        here = slice(at, at + size)
        side = dot(w_s[...], v_ref[:, here], 1, 0)
        total = l_ref[:, here] if acc is None else l_ref[:, here] + acc
        out_ref[:, here] = (scale * total + (side[:rank] + side[rank:])).astype(bf16)

    send_on(0, count // 2, None)
    sweep(kt_ref, u_ref, v_ref, g_ref, ov_ref, send_on, count // 2)


def turn_body(at_ref, ov_ref, got_ref, me_ref, up_ref, dn_ref, away_ref, tot_s):
    tot_s[...] = ov_ref[...].T + got_ref[...].astype(f32)
    rows = me_ref.shape[0]
    y = at_ref[2]

    def part(turn):
        return tot_s[pl.ds(pl.multiple_of(((y + turn) % 4) * rows, rows), rows), :]

    me_ref[...] = part(0)
    up_ref[...] = part(1).astype(bf16)
    away_ref[...] = part(2).astype(bf16)
    dn_ref[...] = part(3).astype(bf16)


def pair_body(at_ref, me_ref, rc_ref, rd_ref, re_ref, mine_ref, send_ref, tot_s):
    rows = mine_ref.shape[0]
    tot_s[...] = (me_ref[...] + rc_ref[...].astype(f32)) + (rd_ref[...].astype(f32) + re_ref[...].astype(f32))
    xh = at_ref[3]
    mine_ref[...] = tot_s[pl.ds(pl.multiple_of(xh * rows, rows), rows), :]
    send_ref[...] = tot_s[pl.ds(pl.multiple_of((1 - xh) * rows, rows), rows), :].astype(bf16)


def done_body(scale, base_ref, mine_ref, *refs):
    parts, out_ref = refs[:-1], refs[-1]
    _, depth, rows, cols = out_ref.shape
    total = mine_ref[...]
    for part in parts:
        total = total + part[...].astype(f32)
    new = base_ref[...] + scale * total
    for x in range(depth):
        for y in range(rows):
            at = (x * rows + y) * cols
            out_ref[:, x, y, :] = new[:, at : at + cols]


def send(x, axis, hops):
    return resident(lax.ppermute(x, axis, hops))


def ring(n, k):
    return [(i, (i + k) % n) for i in range(n)]


def per_device(basis_u, basis_v, core_s, face_class, sample_class):
    narrow, depth_x, rows_y, cols_z = basis_u.shape
    rank = core_s.shape[0]
    n_samp, n_space = 8, 16
    cells = depth_x * rows_y * cols_z
    lanes, samp_rows = basis_v.shape
    half = samp_rows // 2
    cell_weight = rank / (cells * n_space)
    samp_weight = rank / (samp_rows * n_samp)
    core_at = lax.axis_index("c")
    places = (core_at, lax.axis_index(SAMP)) + tuple(lax.axis_index(n) for n in ("y", "xh", "z", "xl"))
    where_at = jnp.stack(places).astype(jnp.int32)
    swap = ring(2, 1)

    u0 = basis_u.reshape(narrow, cells)
    u1 = send(u0, "xh", swap)
    v_half = jnp.transpose(basis_v.reshape(lanes, 2, half), (1, 0, 2))
    v_wide = jnp.broadcast_to(v_half[None], (n_space // 2,) + v_half.shape).reshape(rank, half)
    v = resident(lax.all_to_all(v_wide, SPACE, 0, 0, tiled=True))
    (pair,) = small(functools.partial(stack_body, 3), [resident(u0), u1], [((2 * narrow, cells), bf16, True)], at=where_at)
    around = [send(pair, "y", ring(4, k)) for k in (1, 3, 2)]
    u_own, k_own, kt_own, edge = small(
        prep_body,
        [pair, *around, core_s],
        [((rank, cells), bf16, True), ((rank, cells), bf16, True), ((cells, rank), bf16, True), ((rank, cells // 2), bf16, True)],
        at=where_at,
    )
    u_oth = send(u_own, "c", swap)
    chips = n_space // 2
    hops = [(2 * i + 1, 2 * i + 2) for i in range(chips - 1)] + [(2 * i + 2, 2 * i + 1) for i in range(chips - 1)]
    halo = send(edge, SPACE, hops)

    growth = 0.5 + 0.5 * lax.dynamic_slice_in_dim(sample_class, core_at * half, half, 0).astype(f32)
    growth = resident(growth.reshape(1, half))
    scale = step_size * cell_weight
    l_first, ov_first = small(
        own_body, [kt_own, u_own, v, growth], [((rank, half // 2), f32, True), ((cells, rank), f32, True)]
    )
    kt_oth, base, m_own = small(
        functools.partial(mid_body, rows_y, cols_z),
        [u_oth, core_s, k_own, halo, face_class, u_own],
        [((cells, rank), bf16, True), ((narrow, cells), f32, False), ((rank, rank), f32, True)],
        [((rank, cells), f32), ((rank, cells), bf16)],
        at=where_at,
        held=(ov_first, kt_own, l_first),
    )
    m_oth = send(m_own, "c", swap)
    l_most, ov_send = small(
        oth_body,
        [kt_oth, u_oth, v, growth, l_first],
        [((rank, half), f32, True), ((rank, cells), bf16, True)],
        [((cells, rank), f32)],
        held=(ov_first, kt_own, u_own),
    )
    got = send(ov_send, "c", swap)
    l_part, ov_own = small(
        functools.partial(last_body, scale),
        [kt_own, u_own, v, growth, l_most, ov_first, m_own, m_oth, core_s],
        [((rank, half), bf16, False), ((cells, rank), f32, True)],
        [((2 * rank, rank), bf16)],
    )

    l_got = lax.all_to_all(l_part, SPACE, 0, 0, tiled=True)
    l_new = l_got.reshape(n_space // 2, 2, lanes, half).astype(f32).sum(0)
    l_new = jnp.transpose(l_new, (1, 0, 2)).reshape(lanes, samp_rows)

    rows = rank // 4
    me, up, dn, away = small(
        turn_body,
        [ov_own, got],
        [((rows, cells), f32, True)] + [((rows, cells), bf16, True)] * 3,
        [((rank, cells), f32)],
        at=where_at,
    )
    near = [send(part, "y", ring(4, k)) for part, k in ((up, 1), (dn, 3), (away, 2))]
    mine, rest = small(
        pair_body,
        [me, *near],
        [((narrow, cells), f32, True), ((narrow, cells), bf16, True)],
        [((rows, cells), f32)],
        at=where_at,
    )
    (k_new,) = small(
        functools.partial(done_body, step_size * samp_weight),
        [base, mine, send(rest, "xh", swap)],
        [(basis_u.shape, f32, False)],
    )
    return (k_new, l_new)


def solution(mesh):
    fine = Mesh(mesh.devices.reshape(4, 2, 2, 4, 2), SPACE + SAMP)
    return jax.shard_map(
        per_device,
        mesh=fine,
        in_specs=(P(SAMP, SPACE, None, None), P(SPACE, SAMP), P(), P(None, SPACE, None, None), P(SAMP)),
        out_specs=(P(SAMP, SPACE, None, None), P(SPACE, SAMP)),
        check_vma=False,
    )
```

```python
import functools

import jax
import jax.numpy as jnp
from jax import lax
from jax.experimental import pallas as pl
from jax.experimental.pallas import tpu as pltpu
from jax.sharding import Mesh, PartitionSpec as P

step_size = 0.1
SPACE = ("z", "xl", "c")
SAMP = ("y", "xh")
BLOCK = 2048
bf16, f32 = jnp.bfloat16, jnp.float32


def dot(a, b, ca, cb):
    return lax.dot_general(a, b, (((ca,), (cb,)), ((), ())), preferred_element_type=f32)


def resident(x):
    return pltpu.with_memory_space_constraint(x, pltpu.MemorySpace.VMEM)


def small(body, args, outs, scratch=(), at=None, held=(), limit=24):
    vm = pl.BlockSpec(memory_space=pltpu.VMEM)
    scalars = [] if at is None else [at]
    n_read = len(scalars) + len(args)

    def reading(*refs):
        body(*refs[:n_read], *refs[n_read + len(held) :])

    return pl.pallas_call(
        reading,
        in_specs=[pl.BlockSpec(memory_space=pltpu.SMEM)] * len(scalars)
        + [vm] * (len(args) + len(held)),
        out_specs=[vm] * len(outs),
        out_shape=[(pltpu.VMEM if keep else pltpu.HBM)(shape, dtype) for shape, dtype, keep in outs],
        scratch_shapes=[pltpu.VMEM(shape, dtype) for shape, dtype in scratch],
        compiler_params=pltpu.CompilerParams(vmem_limit_bytes=limit << 20),
    )(*scalars, *args, *held)


def stack_body(which, at_ref, mine_ref, got_ref, *outs):
    rows = mine_ref.shape[0]
    width = outs[0].shape[1]

    def put(top_ref, low_ref):
        for i, out_ref in enumerate(outs):
            out_ref[:rows, :] = top_ref[:, i * width : (i + 1) * width]
            out_ref[rows:, :] = low_ref[:, i * width : (i + 1) * width]

    first = at_ref[which] == 0

    @pl.when(first)
    def _():
        put(mine_ref, got_ref)

    @pl.when(jnp.logical_not(first))
    def _():
        put(got_ref, mine_ref)


def gather_rows(z, pieces, v_ref):
    rows = pieces[0].shape[0]
    for turn, piece in zip((0, 3, 1, 2), pieces):
        v_ref[pl.ds(pl.multiple_of(((z + turn) % 4) * rows, rows), rows), :] = piece[...]


def prep_body(at_ref, p0, p1, p2, p3, core_ref, full_ref, k_ref, kt_ref, halo_ref):
    half = full_ref.shape[1] // 2
    gather_rows(at_ref[2], (p0, p1, p2, p3), full_ref)
    k_own = dot(core_ref[...].astype(bf16), full_ref[...], 0, 0).astype(bf16)
    k_ref[...] = k_own
    kt_ref[...] = k_own.T
    first = at_ref[0] == 0

    @pl.when(first)
    def _():
        halo_ref[...] = k_own[:, :half]

    @pl.when(jnp.logical_not(first))
    def _():
        halo_ref[...] = k_own[:, half:]


def mid_body(rows, cols, c_ref, oth_ref, core_ref, k_ref, halo_ref, face_ref, u_ref, kt_ref, base_ref, m_ref, base_s, lap_s):
    half = oth_ref.shape[1] // 2
    k_oth = dot(core_ref[...].astype(bf16), oth_ref[...], 0, 0).astype(bf16)
    kt_ref[...] = k_oth.T
    first = c_ref[0] == 0
    near = jnp.where(first, k_oth[:, :half].astype(f32), k_oth[:, half:].astype(f32))
    halo = halo_ref[...].astype(f32)
    before = jnp.where(first, halo, near)
    after = jnp.where(first, near, halo)
    plane = rows * cols
    lane = lax.broadcasted_iota(jnp.int32, (1, cols), 1)
    for x in range(2):
        for y in range(rows):
            at = (x * rows + y) * cols
            mid = k_ref[:, at : at + cols].astype(f32)
            w = [0.25 * lax.shift_left(1, face_ref[f, x, y : y + 1, :]).astype(f32) for f in range(6)]
            total = ((w[0] + w[1]) + (w[2] + w[3])) + (w[4] + w[5])
            down = before[:, y * cols : (y + 1) * cols] if x == 0 else k_ref[:, at - plane : at - plane + cols].astype(f32)
            up = after[:, y * cols : (y + 1) * cols] if x == 1 else k_ref[:, at + plane : at + plane + cols].astype(f32)
            out = w[0] * down + w[1] * up - total * mid
            if y > 0:
                out += w[2] * k_ref[:, at - cols : at].astype(f32)
            if y < rows - 1:
                out += w[3] * k_ref[:, at + cols : at + 2 * cols].astype(f32)
            out += jnp.where(lane == 0, 0.0, w[4]) * pltpu.roll(mid, 1, 1)
            out += jnp.where(lane == cols - 1, 0.0, w[5]) * pltpu.roll(mid, cols - 1, 1)
            base_s[:, at : at + cols] = mid + step_size * out
            lap_s[:, at : at + cols] = out.astype(bf16)
    base_ref[...] = base_s[pl.ds(pl.multiple_of(c_ref[1] * base_ref.shape[0], 8), base_ref.shape[0]), :]
    m_ref[...] = dot(u_ref[...], lap_s[...], 1, 1)


def sweep(kt_ref, u_ref, v_ref, g_ref, ov_ref, start, stop, block, store, tile=512):
    def turn(i, _):
        here = pl.ds(pl.multiple_of(start + i * block, block), block)
        v = v_ref[:, here]
        g = g_ref[:, here]
        acc = None
        for row in range(0, u_ref.shape[1], tile):
            field = dot(kt_ref[row : row + tile, :], v, 1, 0)
            react = (field * (g - field * field)).astype(bf16)
            ov_ref[row : row + tile, :] += dot(react, v, 1, 1)
            part = dot(u_ref[:, row : row + tile], react, 1, 0)
            acc = part if acc is None else acc + part
        store(here, acc, v)
        return 0

    lax.fori_loop(0, (stop - start) // block, turn, 0)


def own_body(kt_ref, u_ref, v_ref, g_ref, l_ref, ov_ref):
    ov_ref[...] = jnp.zeros_like(ov_ref)

    def store(here, acc, v):
        l_ref[:, here] = acc

    count = l_ref.shape[1]
    sweep(kt_ref, u_ref, v_ref, g_ref, ov_ref, 0, count, min(BLOCK, count), store)


def oth_body(kt_ref, u_ref, v_ref, g_ref, old_ref, l_ref, send_ref, ov_s):
    ov_s[...] = jnp.zeros_like(ov_s)
    done, count = old_ref.shape[1], l_ref.shape[1]

    def add(here, acc, v):
        l_ref[:, here] = old_ref[:, here] + acc

    def store(here, acc, v):
        l_ref[:, here] = acc

    sweep(kt_ref, u_ref, v_ref, g_ref, ov_s, 0, done, min(BLOCK, done), add)
    sweep(kt_ref, u_ref, v_ref, g_ref, ov_s, done, count, min(BLOCK, count - done), store)
    send_ref[...] = ov_s[...].T.astype(bf16)


def more_body(start, kt_ref, u_ref, v_ref, g_ref, ov_old_ref, l_ref, ov_ref):
    ov_ref[...] = ov_old_ref[...]
    count = l_ref.shape[1]

    def store(here, acc, v):
        l_ref[...] = acc

    sweep(kt_ref, u_ref, v_ref, g_ref, ov_ref, start, start + count, count, store)


def last_body(scale, kt_ref, u_ref, v_ref, g_ref, l_ref, more_ref, ov_old_ref, ma_ref, mb_ref, core_ref, out_ref, ov_ref, w_s):
    rank, count = out_ref.shape
    half = count // 2
    rest = half + more_ref.shape[1]
    ov_ref[...] = ov_old_ref[...]
    w = core_ref[...].astype(bf16).astype(f32) * 0.125 + scale * (ma_ref[...] + mb_ref[...])
    high = w.astype(bf16)
    w_s[:rank, :] = high
    w_s[rank:, :] = (w - high.astype(f32)).astype(bf16)

    def finish(here, total, v):
        side = dot(w_s[...], v, 1, 0)
        out_ref[:, here] = (scale * total + (side[:rank] + side[rank:])).astype(bf16)

    finish(slice(0, half), l_ref[:, :half], v_ref[:, :half])
    finish(slice(half, rest), l_ref[:, half:rest] + more_ref[...], v_ref[:, half:rest])

    def store(here, acc, v):
        finish(here, l_ref[:, here] + acc, v)

    sweep(kt_ref, u_ref, v_ref, g_ref, ov_ref, rest, count, count - rest, store)


def turn_body(at_ref, ov_ref, got_ref, me_ref, up_ref, dn_ref, away_ref, tot_s):
    tot_s[...] = ov_ref[...].T + got_ref[...].astype(f32)
    rows = me_ref.shape[0]
    y = at_ref[2]

    def part(turn):
        return tot_s[pl.ds(pl.multiple_of(((y + turn) % 4) * rows, rows), rows), :]

    me_ref[...] = part(0)
    up_ref[...] = part(1).astype(bf16)
    away_ref[...] = part(2).astype(bf16)
    dn_ref[...] = part(3).astype(bf16)


def pair_body(at_ref, me_ref, rc_ref, rd_ref, re_ref, mine_ref, send_ref, tot_s):
    rows = mine_ref.shape[0]
    tot_s[...] = (me_ref[...] + rc_ref[...].astype(f32)) + (rd_ref[...].astype(f32) + re_ref[...].astype(f32))
    xh = at_ref[3]
    mine_ref[...] = tot_s[pl.ds(pl.multiple_of(xh * rows, rows), rows), :]
    send_ref[...] = tot_s[pl.ds(pl.multiple_of((1 - xh) * rows, rows), rows), :].astype(bf16)


def gain_body(got_ref, out_ref):
    chips, parts, _, half = got_ref.shape
    for p in range(parts):
        total = got_ref[0, p].astype(f32)
        for k in range(1, chips):
            total = total + got_ref[k, p].astype(f32)
        out_ref[:, p * half : (p + 1) * half] = total


def done_body(scale, base_ref, mine_ref, *refs):
    parts, out_ref = refs[:-1], refs[-1]
    _, depth, rows, cols = out_ref.shape
    total = mine_ref[...]
    for part in parts:
        total = total + part[...].astype(f32)
    new = base_ref[...] + scale * total
    for x in range(depth):
        for y in range(rows):
            at = (x * rows + y) * cols
            out_ref[:, x, y, :] = new[:, at : at + cols]


def send(x, axis, hops):
    return resident(lax.ppermute(x, axis, hops))


def ring(n, k):
    return [(i, (i + k) % n) for i in range(n)]


def per_device(basis_u, basis_v, core_s, face_class, sample_class):
    narrow, depth_x, rows_y, cols_z = basis_u.shape
    rank = core_s.shape[0]
    n_samp, n_space = 8, 16
    cells = depth_x * rows_y * cols_z
    lanes, samp_rows = basis_v.shape
    half = samp_rows // 2
    cell_weight = rank / (cells * n_space)
    samp_weight = rank / (samp_rows * n_samp)
    core_at = lax.axis_index("c")
    places = (core_at, lax.axis_index(SAMP)) + tuple(lax.axis_index(n) for n in ("y", "xh", "z", "xl"))
    where_at = jnp.stack(places).astype(jnp.int32)
    swap = ring(2, 1)

    u0 = basis_u.reshape(narrow, cells)
    u1 = send(u0, "xh", swap)
    v_half = jnp.transpose(basis_v.reshape(lanes, 2, half), (1, 0, 2))
    v_wide = jnp.broadcast_to(v_half[None], (n_space // 2,) + v_half.shape).reshape(rank, half)
    v = resident(lax.all_to_all(v_wide, SPACE, 0, 0, tiled=True))
    (pair,) = small(functools.partial(stack_body, 3), [resident(u0), u1], [((2 * narrow, cells), bf16, True)], at=where_at)
    around = [send(pair, "y", ring(4, k)) for k in (1, 3, 2)]
    u_own, k_own, kt_own, edge = small(
        prep_body,
        [pair, *around, core_s],
        [((rank, cells), bf16, True), ((rank, cells), bf16, True), ((cells, rank), bf16, True), ((rank, cells // 2), bf16, True)],
        at=where_at,
    )
    u_oth = send(u_own, "c", swap)
    chips = n_space // 2
    hops = [(2 * i + 1, 2 * i + 2) for i in range(chips - 1)] + [(2 * i + 2, 2 * i + 1) for i in range(chips - 1)]
    halo = send(edge, SPACE, hops)

    growth = 0.5 + 0.5 * lax.dynamic_slice_in_dim(sample_class, core_at * half, half, 0).astype(f32)
    growth = resident(growth.reshape(1, half))
    scale = step_size * cell_weight
    l_first, ov_first = small(
        own_body, [kt_own, u_own, v, growth], [((rank, half // 2), f32, True), ((cells, rank), f32, True)]
    )
    kt_oth, base, m_own = small(
        functools.partial(mid_body, rows_y, cols_z),
        [u_oth, core_s, k_own, halo, face_class, u_own],
        [((cells, rank), bf16, True), ((narrow, cells), f32, True), ((rank, rank), f32, True)],
        [((rank, cells), f32), ((rank, cells), bf16)],
        at=where_at,
        held=(ov_first, kt_own, l_first),
    )
    m_oth = send(m_own, "c", swap)
    l_most, ov_send = small(
        oth_body,
        [kt_oth, u_oth, v, growth, l_first],
        [((rank, half), f32, True), ((rank, cells), bf16, True)],
        [((cells, rank), f32)],
        held=(ov_first, kt_own, u_own, base),
    )
    got = send(ov_send, "c", swap)
    l_more, ov_more = small(
        functools.partial(more_body, half // 2),
        [kt_own, u_own, v, growth, ov_first],
        [((rank, half // 4), f32, True), ((cells, rank), f32, True)],
        held=(l_most, base),
    )
    l_part, ov_own = small(
        functools.partial(last_body, scale),
        [kt_own, u_own, v, growth, l_most, l_more, ov_more, m_own, m_oth, core_s],
        [((rank, half), bf16, False), ((cells, rank), f32, True)],
        [((2 * rank, rank), bf16)],
        held=(base,),
    )

    l_got = lax.all_to_all(l_part, SPACE, 0, 0, tiled=True)
    (l_new,) = small(
        gain_body, [resident(l_got.reshape(n_space // 2, 2, lanes, half))], [((lanes, samp_rows), f32, False)]
    )

    rows = rank // 4
    me, up, dn, away = small(
        turn_body,
        [ov_own, got],
        [((rows, cells), f32, True)] + [((rows, cells), bf16, True)] * 3,
        [((rank, cells), f32)],
        at=where_at,
        held=(base,),
    )
    near = [send(part, "y", ring(4, k)) for part, k in ((up, 1), (dn, 3), (away, 2))]
    mine, rest = small(
        pair_body,
        [me, *near],
        [((narrow, cells), f32, True), ((narrow, cells), bf16, True)],
        [((rows, cells), f32)],
        at=where_at,
        held=(base,),
    )
    (k_new,) = small(
        functools.partial(done_body, step_size * samp_weight),
        [base, mine, send(rest, "xh", swap)],
        [(basis_u.shape, f32, False)],
    )
    return (k_new, l_new)


def solution(mesh):
    fine = Mesh(mesh.devices.reshape(4, 2, 2, 4, 2), SPACE + SAMP)
    return jax.shard_map(
        per_device,
        mesh=fine,
        in_specs=(P(SAMP, SPACE, None, None), P(SPACE, SAMP), P(), P(None, SPACE, None, None), P(SAMP)),
        out_specs=(P(SAMP, SPACE, None, None), P(SPACE, SAMP)),
        check_vma=False,
    )
```

```python
import functools

import jax
import jax.numpy as jnp
from jax import lax
from jax.experimental import pallas as pl
from jax.experimental.pallas import tpu as pltpu
from jax.sharding import Mesh, PartitionSpec as P

step_size = 0.1
SPACE = ("z", "xl", "c")
SAMP = ("y", "xh")
BLOCK = 2048
bf16, f32 = jnp.bfloat16, jnp.float32


def dot(a, b, ca, cb):
    return lax.dot_general(a, b, (((ca,), (cb,)), ((), ())), preferred_element_type=f32)


def resident(x):
    return pltpu.with_memory_space_constraint(x, pltpu.MemorySpace.VMEM)


def small(body, args, outs, scratch=(), at=None, held=(), limit=24):
    vm = pl.BlockSpec(memory_space=pltpu.VMEM)
    scalars = [] if at is None else [at]
    n_read = len(scalars) + len(args)

    def reading(*refs):
        body(*refs[:n_read], *refs[n_read + len(held) :])

    return pl.pallas_call(
        reading,
        in_specs=[pl.BlockSpec(memory_space=pltpu.SMEM)] * len(scalars)
        + [vm] * (len(args) + len(held)),
        out_specs=[vm] * len(outs),
        out_shape=[(pltpu.VMEM if keep else pltpu.HBM)(shape, dtype) for shape, dtype, keep in outs],
        scratch_shapes=[pltpu.VMEM(shape, dtype) for shape, dtype in scratch],
        compiler_params=pltpu.CompilerParams(vmem_limit_bytes=limit << 20),
    )(*scalars, *args, *held)


def fan_body(v_hbm, out_hbm, v_s, read_sem, sems):
    chips, parts, _, half = out_hbm.shape
    read = pltpu.make_async_copy(v_hbm, v_s, read_sem)
    read.start()
    read.wait()
    writes = [
        pltpu.make_async_copy(v_s.at[:, p * half : (p + 1) * half], out_hbm.at[k, p], sems.at[k * parts + p])
        for k in range(chips)
        for p in range(parts)
    ]
    for write in writes:
        write.start()
    for write in writes:
        write.wait()


def prep_body(at_ref, u_ref, w_ref, a_ref, b_ref, c_ref, core_ref, full_ref, k_ref, kt_ref, halo_ref):
    narrow, cells = u_ref.shape
    half = cells // 2
    y, xh = at_ref[2], at_ref[3]

    def put(turn, flip, value):
        row = (((y + turn) % 4) * 2 + (xh if flip == 0 else 1 - xh)) * narrow
        full_ref[pl.ds(pl.multiple_of(row, narrow), narrow), :] = value

    put(0, 0, u_ref[...])
    put(0, 1, w_ref[...])
    for turn, ref in ((3, a_ref), (1, b_ref), (2, c_ref)):
        put(turn, 0, ref[:narrow, :])
        put(turn, 1, ref[narrow:, :])
    k_own = dot(core_ref[...].astype(bf16), full_ref[...], 0, 0).astype(bf16)
    k_ref[...] = k_own
    kt_ref[...] = k_own.T
    first = at_ref[0] == 0

    @pl.when(first)
    def _():
        halo_ref[...] = k_own[:, :half]

    @pl.when(jnp.logical_not(first))
    def _():
        halo_ref[...] = k_own[:, half:]


def other_body(at_ref, oth_ref, core_ref, kt_ref, near_ref):
    half = near_ref.shape[1]
    k_oth = dot(core_ref[...].astype(bf16), oth_ref[...], 0, 0).astype(bf16)
    kt_ref[...] = k_oth.T
    first = at_ref[0] == 0

    @pl.when(first)
    def _():
        near_ref[...] = k_oth[:, :half]

    @pl.when(jnp.logical_not(first))
    def _():
        near_ref[...] = k_oth[:, half:]


def lap_body(rows, cols, c_ref, near_ref, k_ref, halo_ref, face_ref, u_ref, base_ref, m_ref, base_s, lap_s):
    first = c_ref[0] == 0
    near = near_ref[...].astype(f32)
    halo = halo_ref[...].astype(f32)
    before = jnp.where(first, halo, near)
    after = jnp.where(first, near, halo)
    plane = rows * cols
    lane = lax.broadcasted_iota(jnp.int32, (1, cols), 1)
    for x in range(2):
        for y in range(rows):
            at = (x * rows + y) * cols
            mid = k_ref[:, at : at + cols].astype(f32)
            w = [0.25 * lax.shift_left(1, face_ref[f, x, y : y + 1, :]).astype(f32) for f in range(6)]
            total = ((w[0] + w[1]) + (w[2] + w[3])) + (w[4] + w[5])
            down = before[:, y * cols : (y + 1) * cols] if x == 0 else k_ref[:, at - plane : at - plane + cols].astype(f32)
            up = after[:, y * cols : (y + 1) * cols] if x == 1 else k_ref[:, at + plane : at + plane + cols].astype(f32)
            out = w[0] * down + w[1] * up - total * mid
            if y > 0:
                out += w[2] * k_ref[:, at - cols : at].astype(f32)
            if y < rows - 1:
                out += w[3] * k_ref[:, at + cols : at + 2 * cols].astype(f32)
            out += jnp.where(lane == 0, 0.0, w[4]) * pltpu.roll(mid, 1, 1)
            out += jnp.where(lane == cols - 1, 0.0, w[5]) * pltpu.roll(mid, cols - 1, 1)
            base_s[:, at : at + cols] = mid + step_size * out
            lap_s[:, at : at + cols] = out.astype(bf16)
    base_ref[...] = base_s[pl.ds(pl.multiple_of(c_ref[1] * base_ref.shape[0], 8), base_ref.shape[0]), :]
    m_ref[...] = dot(u_ref[...], lap_s[...], 1, 1)


def sweep(kt_ref, u_ref, v_ref, g_ref, ov_ref, start, stop, store, tile=512):
    block = min(BLOCK, stop - start)

    def turn(i, _):
        at = pl.multiple_of(start + i * block, block)
        v = v_ref[:, pl.ds(at, block)]
        g = g_ref[:, pl.ds(at, block)]
        acc = None
        for row in range(0, u_ref.shape[1], tile):
            field = dot(kt_ref[row : row + tile, :], v, 1, 0)
            react = (field * (g - field * field)).astype(bf16)
            ov_ref[row : row + tile, :] += dot(react, v, 1, 1)
            part = dot(u_ref[:, row : row + tile], react, 1, 0)
            acc = part if acc is None else acc + part
        store(pl.ds(pl.multiple_of(at - start, block), block), acc)
        return 0

    lax.fori_loop(0, (stop - start) // block, turn, 0)


def part_body(start, has_old, back, kt_ref, u_ref, v_ref, g_ref, *refs):
    refs = list(refs)
    old_ref = refs.pop(0) if has_old & 1 else None
    far_ref = refs.pop(0) if has_old & 2 else None
    l_ref, ov_ref = refs[:2]
    ov_s = refs[2] if back else ov_ref
    ov_s[...] = jnp.zeros_like(ov_s) if far_ref is None else far_ref[...]

    def store(here, acc):
        l_ref[:, here] = acc if old_ref is None else old_ref[:, here] + acc

    stop = start + l_ref.shape[1]
    done = 0 if old_ref is None else old_ref.shape[1]
    if done:
        sweep(kt_ref, u_ref, v_ref, g_ref, ov_s, start, start + done, store)
    if start + done < stop:

        def rest(here, acc):
            l_ref[:, pl.ds(pl.multiple_of(here.start + done, done or BLOCK), here.size)] = acc

        sweep(kt_ref, u_ref, v_ref, g_ref, ov_s, start + done, stop, rest)
    if back:
        ov_ref[...] = ov_s[...].T.astype(bf16)


def last_body(
    scale, at_ref, kt_ref, u_ref, v_ref, g_ref, l_ref, more_ref, ov_ref, got_ref, ma_ref, mb_ref, core_ref,
    out_ref, me_ref, up_ref, dn_ref, away_ref, ov_s, tot_s, w_s,
):
    rank, count = out_ref.shape
    middle = count - count // 2
    start = middle + more_ref.shape[1]
    ov_s[...] = ov_ref[...]
    w = core_ref[...].astype(bf16).astype(f32) * 0.125 + scale * (ma_ref[...] + mb_ref[...])
    high = w.astype(bf16)
    w_s[:rank, :] = high
    w_s[rank:, :] = (w - high.astype(f32)).astype(bf16)

    def send(at, size, total):
        side = dot(w_s[...], v_ref[:, at : at + size], 1, 0)
        out_ref[:, at : at + size] = (scale * total + (side[:rank] + side[rank:])).astype(bf16)

    send(0, middle, l_ref[:, :middle])
    send(middle, start - middle, l_ref[:, middle:start] + more_ref[...])

    def store(here, acc):
        send(start, count - start, l_ref[:, start:] + acc)

    sweep(kt_ref, u_ref, v_ref, g_ref, ov_s, start, count, store)
    tot_s[...] = ov_s[...].T + got_ref[...].astype(f32)
    rows = me_ref.shape[0]
    y = at_ref[2]

    def part(turn):
        return tot_s[pl.ds(pl.multiple_of(((y + turn) % 4) * rows, rows), rows), :]

    me_ref[...] = part(0)
    up_ref[...] = part(1).astype(bf16)
    away_ref[...] = part(2).astype(bf16)
    dn_ref[...] = part(3).astype(bf16)


def done_body(scale, base_ref, mine_ref, got_ref, out_ref):
    _, depth, rows, cols = out_ref.shape
    new = base_ref[...] + scale * (mine_ref[...] + got_ref[...].astype(f32))
    for x in range(depth):
        for y in range(rows):
            at = (x * rows + y) * cols
            out_ref[:, x, y, :] = new[:, at : at + cols]


def pair_body(at_ref, me_ref, rc_ref, rd_ref, re_ref, mine_ref, send_ref, tot_s):
    rows = mine_ref.shape[0]
    tot_s[...] = (me_ref[...] + rc_ref[...].astype(f32)) + (rd_ref[...].astype(f32) + re_ref[...].astype(f32))
    xh = at_ref[3]
    mine_ref[...] = tot_s[pl.ds(pl.multiple_of(xh * rows, rows), rows), :]
    send_ref[...] = tot_s[pl.ds(pl.multiple_of((1 - xh) * rows, rows), rows), :].astype(bf16)


def ring(n, k):
    return [(i, (i + k) % n) for i in range(n)]


def per_device(basis_u, basis_v, core_s, face_class, sample_class):
    narrow, depth_x, rows_y, cols_z = basis_u.shape
    rank = core_s.shape[0]
    n_samp, n_space = 8, 16
    cells = depth_x * rows_y * cols_z
    lanes, samp_rows = basis_v.shape
    half = samp_rows // 2
    cell_weight = rank / (cells * n_space)
    samp_weight = rank / (samp_rows * n_samp)
    core_at = lax.axis_index("c")
    where_at = jnp.stack([core_at, lax.axis_index(SAMP), lax.axis_index("y"), lax.axis_index("xh")]).astype(jnp.int32)
    swap = ring(2, 1)

    u0 = basis_u.reshape(narrow, cells)
    anywhere = pl.BlockSpec(memory_space=pl.ANY)
    v_wide = pl.pallas_call(
        fan_body,
        in_specs=[anywhere],
        out_specs=anywhere,
        out_shape=jax.ShapeDtypeStruct((n_space // 2, 2, lanes, half), bf16),
        scratch_shapes=[
            pltpu.VMEM(basis_v.shape, bf16),
            pltpu.SemaphoreType.DMA,
            pltpu.SemaphoreType.DMA((n_space,)),
        ],
    )(basis_v)
    v = resident(lax.all_to_all(v_wide.reshape(rank, half), SPACE, 0, 0, tiled=True))
    u1 = lax.ppermute(u0, "xh", swap)
    pair = jnp.concatenate([u0, u1], 0)
    around = [resident(lax.ppermute(pair, "y", ring(4, k))) for k in (1, 3, 2)]
    u_own, k_own, kt_own, edge = small(
        prep_body,
        [resident(u0), resident(u1), *around, core_s],
        [((rank, cells), bf16, True), ((rank, cells), bf16, True), ((cells, rank), bf16, True), ((rank, cells // 2), bf16, True)],
        at=where_at,
    )
    u_oth = resident(lax.ppermute(u_own, "c", swap))
    chips = n_space // 2
    hops = [(2 * i + 1, 2 * i + 2) for i in range(chips - 1)] + [(2 * i + 2, 2 * i + 1) for i in range(chips - 1)]
    halo = resident(lax.ppermute(edge, SPACE, hops))

    growth = 0.5 + 0.5 * lax.dynamic_slice_in_dim(sample_class, core_at * half, half, 0).astype(f32)
    growth = resident(growth.reshape(1, half))
    scale = step_size * cell_weight
    quart = half // 2
    main = lambda start, kinds, back: functools.partial(part_body, start, kinds, back)
    kt_oth, near = small(
        other_body,
        [u_oth, core_s],
        [((cells, rank), bf16, True), ((rank, cells // 2), bf16, True)],
        at=where_at,
        held=(k_own, kt_own, u_own),
    )
    l_first, ov_first = small(
        main(0, 0, False),
        [kt_own, u_own, v, growth],
        [((rank, quart), f32, True), ((cells, rank), f32, True)],
        held=(kt_oth, near, k_own),
    )
    base, m_own = small(
        functools.partial(lap_body, rows_y, cols_z),
        [near, k_own, halo, face_class, u_own],
        [((narrow, cells), f32, False), ((rank, rank), f32, True)],
        [((rank, cells), f32), ((rank, cells), bf16)],
        at=where_at,
        held=(ov_first, kt_own, l_first, kt_oth, u_oth),
    )
    m_oth = resident(lax.ppermute(m_own, "c", swap))
    l_most, ov_send = small(
        main(0, 1, True),
        [kt_oth, u_oth, v, growth, l_first],
        [((rank, half), f32, True), ((rank, cells), bf16, True)],
        [((cells, rank), f32)],
        held=(ov_first, kt_own, u_own, m_own),
    )
    got = resident(lax.ppermute(ov_send, "c", swap))
    l_more, ov_more = small(
        main(quart, 2, False),
        [kt_own, u_own, v, growth, ov_first],
        [((rank, quart // 2), f32, True), ((cells, rank), f32, True)],
        held=(l_most, ov_send, m_own),
    )
    rows = rank // 4
    l_part, me, up, dn, away = small(
        functools.partial(last_body, scale),
        [kt_own, u_own, v, growth, l_most, l_more, ov_more, got, m_own, m_oth, core_s],
        [((rank, half), bf16, False), ((rows, cells), f32, True)] + [((rows, cells), bf16, True)] * 3,
        [((cells, rank), f32), ((rank, cells), f32), ((2 * rank, rank), bf16)],
        at=where_at,
    )

    l_got = lax.all_to_all(l_part, SPACE, 0, 0, tiled=True)
    l_new = l_got.reshape(n_space // 2, 2, lanes, half).astype(f32).sum(0)
    l_new = jnp.transpose(l_new, (1, 0, 2)).reshape(lanes, samp_rows)

    near = [resident(lax.ppermute(part, "y", ring(4, k))) for part, k in ((up, 1), (dn, 3), (away, 2))]
    mine, send = small(
        pair_body,
        [me, *near],
        [((narrow, cells), f32, True), ((narrow, cells), bf16, True)],
        [((rows, cells), f32)],
        at=where_at,
    )
    (k_new,) = small(
        functools.partial(done_body, step_size * samp_weight),
        [base, mine, resident(lax.ppermute(send, "xh", swap))],
        [(basis_u.shape, f32, False)],
    )
    return (k_new, l_new)


def solution(mesh):
    fine = Mesh(mesh.devices.reshape(4, 2, 2, 4, 2), SPACE + SAMP)
    return jax.shard_map(
        per_device,
        mesh=fine,
        in_specs=(P(SAMP, SPACE, None, None), P(SPACE, SAMP), P(), P(None, SPACE, None, None), P(SAMP)),
        out_specs=(P(SAMP, SPACE, None, None), P(SPACE, SAMP)),
        check_vma=False,
    )
```

```python
import functools

import jax
import jax.numpy as jnp
from jax import lax
from jax.experimental import pallas as pl
from jax.experimental.pallas import tpu as pltpu
from jax.sharding import Mesh, PartitionSpec as P

step_size = 0.1
SPACE = ("z", "xl", "c")
SAMP = ("y", "xh")
bf16, f32 = jnp.bfloat16, jnp.float32


def dot(a, b, ca, cb):
    return lax.dot_general(a, b, (((ca,), (cb,)), ((), ())), preferred_element_type=f32)


def resident(x):
    return pltpu.with_memory_space_constraint(x, pltpu.MemorySpace.VMEM)


def small(body, args, outs, scratch=(), at=None, held=(), limit=24):
    vm = pl.BlockSpec(memory_space=pltpu.VMEM)
    scalars = [] if at is None else [at]
    n_read = len(scalars) + len(args)

    def reading(*refs):
        body(*refs[:n_read], *refs[n_read + len(held) :])

    return pl.pallas_call(
        reading,
        in_specs=[pl.BlockSpec(memory_space=pltpu.SMEM)] * len(scalars)
        + [vm] * (len(args) + len(held)),
        out_specs=[vm] * len(outs),
        out_shape=[(pltpu.VMEM if keep else pltpu.HBM)(shape, dtype) for shape, dtype, keep in outs],
        scratch_shapes=[pltpu.VMEM(shape, dtype) for shape, dtype in scratch],
        compiler_params=pltpu.CompilerParams(vmem_limit_bytes=limit << 20),
    )(*scalars, *args, *held)


def head_body(u_ref, v_ref, flat_ref, out_ref, u_s):
    _, depth, rows, cols = u_ref.shape
    u_s[...] = u_ref[...].astype(f32)
    for x in range(depth):
        for y in range(rows):
            at = (x * rows + y) * cols
            flat_ref[:, at : at + cols] = u_s[:, x, y, :].astype(bf16)
    half = out_ref.shape[-1]
    for k in range(out_ref.shape[0]):
        out_ref[k, 0] = v_ref[:, :half]
        out_ref[k, 1] = v_ref[:, half:]


def prep_body(at_ref, u_ref, w_ref, a_ref, b_ref, c_ref, core_ref, full_ref, k_ref, kt_ref, halo_ref):
    narrow, cells = u_ref.shape
    half = cells // 2
    y, xh = at_ref[2], at_ref[3]

    def put(turn, flip, value):
        row = (((y + turn) % 4) * 2 + (xh if flip == 0 else 1 - xh)) * narrow
        full_ref[pl.ds(pl.multiple_of(row, narrow), narrow), :] = value

    put(0, 0, u_ref[...])
    put(0, 1, w_ref[...])
    for turn, ref in ((3, a_ref), (1, b_ref), (2, c_ref)):
        put(turn, 0, ref[:narrow, :])
        put(turn, 1, ref[narrow:, :])
    k_own = dot(core_ref[...].astype(bf16), full_ref[...], 0, 0).astype(bf16)
    k_ref[...] = k_own
    kt_ref[...] = k_own.T
    first = at_ref[0] == 0

    @pl.when(first)
    def _():
        halo_ref[...] = k_own[:, :half]

    @pl.when(jnp.logical_not(first))
    def _():
        halo_ref[...] = k_own[:, half:]


def mid_body(rows, cols, c_ref, oth_ref, core_ref, k_ref, halo_ref, face_ref, u_ref, kt_ref, base_ref, m_ref, base_s, lap_s, w_s, k_s):
    half = oth_ref.shape[1] // 2
    k_oth = dot(core_ref[...].astype(bf16), oth_ref[...], 0, 0).astype(bf16)
    kt_ref[...] = k_oth.T
    first = c_ref[0] == 0
    near = jnp.where(first, k_oth[:, :half].astype(f32), k_oth[:, half:].astype(f32))
    halo = halo_ref[...].astype(f32)
    before = jnp.where(first, halo, near)
    after = jnp.where(first, near, halo)
    plane = rows * cols
    lane = lax.broadcasted_iota(jnp.int32, (1, 1, cols), 2)
    faces = [0.25 * lax.shift_left(1, face_ref[f]).astype(f32) for f in range(6)]
    w_s[6] = ((faces[0] + faces[1]) + (faces[2] + faces[3])) + (faces[4] + faces[5])
    faces[4] = jnp.where(lane == 0, 0.0, faces[4])
    faces[5] = jnp.where(lane == cols - 1, 0.0, faces[5])
    for f in range(6):
        w_s[f] = faces[f]
    k_s[...] = k_ref[...].astype(f32)
    for x in range(2):
        for y in range(rows):
            at = (x * rows + y) * cols
            mid = k_s[:, at : at + cols]
            w = [w_s[f, x, y : y + 1, :] for f in range(7)]
            down = before[:, y * cols : (y + 1) * cols] if x == 0 else k_s[:, at - plane : at - plane + cols]
            up = after[:, y * cols : (y + 1) * cols] if x == 1 else k_s[:, at + plane : at + plane + cols]
            out = w[0] * down + w[1] * up - w[6] * mid
            if y > 0:
                out += w[2] * k_s[:, at - cols : at]
            if y < rows - 1:
                out += w[3] * k_s[:, at + cols : at + 2 * cols]
            out += w[4] * pltpu.roll(mid, 1, 1)
            out += w[5] * pltpu.roll(mid, cols - 1, 1)
            base_s[:, at : at + cols] = mid + step_size * out
            lap_s[:, at : at + cols] = out.astype(bf16)
    base_ref[...] = base_s[pl.ds(pl.multiple_of(c_ref[1] * base_ref.shape[0], 8), base_ref.shape[0]), :]
    m_ref[...] = dot(u_ref[...], lap_s[...], 1, 1)


def sweep(kt_ref, u_ref, v_ref, g_ref, ov_ref, start, stop, store, tile=512):
    block = stop - start

    def turn(i, _):
        at = pl.multiple_of(start + i * block, block)
        v = v_ref[:, pl.ds(at, block)]
        g = g_ref[:, pl.ds(at, block)]
        acc = None
        for row in range(0, u_ref.shape[1], tile):
            field = dot(kt_ref[row : row + tile, :], v, 1, 0)
            react = (field * (g - field * field)).astype(bf16)
            ov_ref[row : row + tile, :] += dot(react, v, 1, 1)
            part = dot(u_ref[:, row : row + tile], react, 1, 0)
            acc = part if acc is None else acc + part
        store(pl.ds(pl.multiple_of(at - start, block), block), acc)
        return 0

    lax.fori_loop(0, (stop - start) // block, turn, 0)


def part_body(start, has_old, back, kt_ref, u_ref, v_ref, g_ref, *refs):
    refs = list(refs)
    old_ref = refs.pop(0) if has_old & 1 else None
    far_ref = refs.pop(0) if has_old & 2 else None
    l_ref, ov_ref = refs[:2]
    ov_s = refs[2] if back else ov_ref
    ov_s[...] = jnp.zeros_like(ov_s) if far_ref is None else far_ref[...]

    done = 0 if old_ref is None else old_ref.shape[1]

    def store(here, acc):
        if done:
            l_ref[:, :done] = old_ref[...] + acc[:, :done]
            l_ref[:, done:] = acc[:, done:]
        else:
            l_ref[:, here] = acc

    sweep(kt_ref, u_ref, v_ref, g_ref, ov_s, start, start + l_ref.shape[1], store)
    if back:
        ov_ref[...] = ov_s[...].T.astype(bf16)


def last_body(
    scale, at_ref, kt_ref, u_ref, v_ref, g_ref, l_ref, more_ref, ov_ref, got_ref, ma_ref, mb_ref, core_ref,
    out_ref, me_ref, up_ref, dn_ref, away_ref, ov_s, tot_s, w_s,
):
    rank, count = out_ref.shape
    middle = count - count // 2
    start = middle + more_ref.shape[1]
    ov_s[...] = ov_ref[...]
    w = core_ref[...].astype(bf16).astype(f32) * 0.125 + scale * (ma_ref[...] + mb_ref[...])
    high = w.astype(bf16)
    w_s[:rank, :] = high
    w_s[rank:, :] = (w - high.astype(f32)).astype(bf16)

    def send(at, size, total):
        side = dot(w_s[...], v_ref[:, at : at + size], 1, 0)
        out_ref[:, at : at + size] = (scale * total + (side[:rank] + side[rank:])).astype(bf16)

    send(0, middle, l_ref[:, :middle])
    send(middle, start - middle, l_ref[:, middle:start] + more_ref[...])

    def store(here, acc):
        send(start, count - start, l_ref[:, start:] + acc)

    sweep(kt_ref, u_ref, v_ref, g_ref, ov_s, start, count, store)
    tot_s[...] = ov_s[...].T + got_ref[...].astype(f32)
    rows = me_ref.shape[0]
    y = at_ref[2]

    def part(turn):
        return tot_s[pl.ds(pl.multiple_of(((y + turn) % 4) * rows, rows), rows), :]

    me_ref[...] = part(0)
    up_ref[...] = part(1).astype(bf16)
    away_ref[...] = part(2).astype(bf16)
    dn_ref[...] = part(3).astype(bf16)


def done_body(scale, base_ref, mine_ref, got_ref, out_ref):
    _, depth, rows, cols = out_ref.shape
    new = base_ref[...] + scale * (mine_ref[...] + got_ref[...].astype(f32))
    for x in range(depth):
        for y in range(rows):
            at = (x * rows + y) * cols
            out_ref[:, x, y, :] = new[:, at : at + cols]


def pair_body(at_ref, me_ref, rc_ref, rd_ref, re_ref, mine_ref, send_ref, tot_s):
    rows = mine_ref.shape[0]
    tot_s[...] = (me_ref[...] + rc_ref[...].astype(f32)) + (rd_ref[...].astype(f32) + re_ref[...].astype(f32))
    xh = at_ref[3]
    mine_ref[...] = tot_s[pl.ds(pl.multiple_of(xh * rows, rows), rows), :]
    send_ref[...] = tot_s[pl.ds(pl.multiple_of((1 - xh) * rows, rows), rows), :].astype(bf16)


def ring(n, k):
    return [(i, (i + k) % n) for i in range(n)]


def per_device(basis_u, basis_v, core_s, face_class, sample_class):
    narrow, depth_x, rows_y, cols_z = basis_u.shape
    rank = core_s.shape[0]
    n_samp, n_space = 8, 16
    cells = depth_x * rows_y * cols_z
    lanes, samp_rows = basis_v.shape
    half = samp_rows // 2
    cell_weight = rank / (cells * n_space)
    samp_weight = rank / (samp_rows * n_samp)
    core_at = lax.axis_index("c")
    where_at = jnp.stack([core_at, lax.axis_index(SAMP), lax.axis_index("y"), lax.axis_index("xh")]).astype(jnp.int32)
    swap = ring(2, 1)

    u0, v_wide = small(
        head_body,
        [basis_u, basis_v],
        [((narrow, cells), bf16, True), ((n_space // 2, 2, lanes, half), bf16, False)],
        [(basis_u.shape, f32)],
    )
    v = resident(lax.all_to_all(v_wide.reshape(rank, half), SPACE, 0, 0, tiled=True))
    u1 = lax.ppermute(u0, "xh", swap)
    pair = jnp.concatenate([u0, u1], 0)
    around = [resident(lax.ppermute(pair, "y", ring(4, k))) for k in (1, 3, 2)]
    u_own, k_own, kt_own, edge = small(
        prep_body,
        [u0, resident(u1), *around, core_s],
        [((rank, cells), bf16, True), ((rank, cells), bf16, True), ((cells, rank), bf16, True), ((rank, cells // 2), bf16, True)],
        at=where_at,
    )
    u_oth = resident(lax.ppermute(u_own, "c", swap))
    chips = n_space // 2
    hops = [(2 * i + 1, 2 * i + 2) for i in range(chips - 1)] + [(2 * i + 2, 2 * i + 1) for i in range(chips - 1)]
    halo = resident(lax.ppermute(edge, SPACE, hops))

    growth = 0.5 + 0.5 * lax.dynamic_slice_in_dim(sample_class, core_at * half, half, 0).astype(f32)
    growth = resident(growth.reshape(1, half))
    scale = step_size * cell_weight
    quart = half // 2
    main = lambda start, kinds, back: functools.partial(part_body, start, kinds, back)
    l_first, ov_first = small(
        main(0, 0, False), [kt_own, u_own, v, growth], [((rank, quart), f32, True), ((cells, rank), f32, True)]
    )
    kt_oth, base, m_own = small(
        functools.partial(mid_body, rows_y, cols_z),
        [u_oth, core_s, k_own, halo, face_class, u_own],
        [((cells, rank), bf16, True), ((narrow, cells), f32, False), ((rank, rank), f32, True)],
        [((rank, cells), f32), ((rank, cells), bf16), ((7,) + face_class.shape[1:], f32), ((rank, cells), f32)],
        at=where_at,
        held=(ov_first, kt_own, l_first),
    )
    m_oth = resident(lax.ppermute(m_own, "c", swap))
    l_most, ov_send = small(
        main(0, 1, True),
        [kt_oth, u_oth, v, growth, l_first],
        [((rank, half), f32, True), ((rank, cells), bf16, True)],
        [((cells, rank), f32)],
        held=(ov_first, kt_own, u_own),
    )
    got = resident(lax.ppermute(ov_send, "c", swap))
    l_more, ov_more = small(
        main(quart, 2, False),
        [kt_own, u_own, v, growth, ov_first],
        [((rank, quart // 2), f32, True), ((cells, rank), f32, True)],
        held=(l_most, ov_send),
    )
    rows = rank // 4
    l_part, me, up, dn, away = small(
        functools.partial(last_body, scale),
        [kt_own, u_own, v, growth, l_most, l_more, ov_more, got, m_own, m_oth, core_s],
        [((rank, half), bf16, False), ((rows, cells), f32, True)] + [((rows, cells), bf16, True)] * 3,
        [((cells, rank), f32), ((rank, cells), f32), ((2 * rank, rank), bf16)],
        at=where_at,
    )

    l_got = lax.all_to_all(l_part, SPACE, 0, 0, tiled=True)
    l_new = l_got.reshape(n_space // 2, 2, lanes, half).astype(f32).sum(0)
    l_new = jnp.transpose(l_new, (1, 0, 2)).reshape(lanes, samp_rows)

    near = []
    for part, k in ((up, 1), (dn, 3), (away, 2)):
        near.append(resident(lax.ppermute(part, "y", ring(4, k))))
    mine, send = small(
        pair_body,
        [me, *near],
        [((narrow, cells), f32, True), ((narrow, cells), bf16, True)],
        [((rows, cells), f32)],
        at=where_at,
    )
    (k_new,) = small(
        functools.partial(done_body, step_size * samp_weight),
        [base, mine, resident(lax.ppermute(send, "xh", swap))],
        [(basis_u.shape, f32, False)],
    )
    return (k_new, l_new)


def solution(mesh):
    fine = Mesh(mesh.devices.reshape(4, 2, 2, 4, 2), SPACE + SAMP)
    return jax.shard_map(
        per_device,
        mesh=fine,
        in_specs=(P(SAMP, SPACE, None, None), P(SPACE, SAMP), P(), P(None, SPACE, None, None), P(SAMP)),
        out_specs=(P(SAMP, SPACE, None, None), P(SPACE, SAMP)),
        check_vma=False,
    )
```

```python
import functools

import jax
import jax.numpy as jnp
from jax import lax
from jax.experimental import pallas as pl
from jax.experimental.pallas import tpu as pltpu
from jax.sharding import Mesh, PartitionSpec as P

step_size = 0.1
SPACE = ("z", "xl", "c")
SAMP = ("y", "xh")
bf16, f32 = jnp.bfloat16, jnp.float32


def dot(a, b, ca, cb):
    return lax.dot_general(a, b, (((ca,), (cb,)), ((), ())), preferred_element_type=f32)


def resident(x):
    return pltpu.with_memory_space_constraint(x, pltpu.MemorySpace.VMEM)


def small(body, args, outs, scratch=(), at=None, held=(), limit=24):
    vm = pl.BlockSpec(memory_space=pltpu.VMEM)
    scalars = [] if at is None else [at]
    n_read = len(scalars) + len(args)

    def reading(*refs):
        body(*refs[:n_read], *refs[n_read + len(held) :])

    return pl.pallas_call(
        reading,
        in_specs=[pl.BlockSpec(memory_space=pltpu.SMEM)] * len(scalars)
        + [vm] * (len(args) + len(held)),
        out_specs=[vm] * len(outs),
        out_shape=[(pltpu.VMEM if keep else pltpu.HBM)(shape, dtype) for shape, dtype, keep in outs],
        scratch_shapes=[pltpu.VMEM(shape, dtype) for shape, dtype in scratch],
        compiler_params=pltpu.CompilerParams(vmem_limit_bytes=limit << 20),
    )(*scalars, *args, *held)


def fan_body(v_ref, out_ref):
    half = out_ref.shape[-1]
    for k in range(out_ref.shape[0]):
        out_ref[k, 0] = v_ref[:, :half]
        out_ref[k, 1] = v_ref[:, half:]


def flat_body(own_ref, got_ref, out_ref, u_s):
    narrow, depth, rows, cols = own_ref.shape
    for i, ref in enumerate((own_ref, got_ref)):
        u_s[...] = ref[...].astype(f32)
        for x in range(depth):
            for y in range(rows):
                at = (x * rows + y) * cols
                out_ref[i * narrow : (i + 1) * narrow, at : at + cols] = u_s[:, x, y, :].astype(bf16)


def prep_body(at_ref, u_ref, a_ref, b_ref, c_ref, core_ref, full_ref, k_ref, kt_ref, halo_ref):
    narrow, cells = u_ref.shape[0] // 2, u_ref.shape[1]
    half = cells // 2
    y, xh = at_ref[2], at_ref[3]

    def put(turn, flip, value):
        row = (((y + turn) % 4) * 2 + (xh if flip == 0 else 1 - xh)) * narrow
        full_ref[pl.ds(pl.multiple_of(row, narrow), narrow), :] = value

    for turn, ref in ((0, u_ref), (3, a_ref), (1, b_ref), (2, c_ref)):
        put(turn, 0, ref[:narrow, :])
        put(turn, 1, ref[narrow:, :])
    k_own = dot(core_ref[...].astype(bf16), full_ref[...], 0, 0).astype(bf16)
    k_ref[...] = k_own
    kt_ref[...] = k_own.T
    first = at_ref[0] == 0

    @pl.when(first)
    def _():
        halo_ref[...] = k_own[:, :half]

    @pl.when(jnp.logical_not(first))
    def _():
        halo_ref[...] = k_own[:, half:]


def mid_body(rows, cols, c_ref, oth_ref, core_ref, k_ref, halo_ref, face_ref, u_ref, kt_ref, base_ref, m_ref, base_s, lap_s, w_s, k_s):
    half = oth_ref.shape[1] // 2
    k_oth = dot(core_ref[...].astype(bf16), oth_ref[...], 0, 0).astype(bf16)
    kt_ref[...] = k_oth.T
    first = c_ref[0] == 0
    near = jnp.where(first, k_oth[:, :half].astype(f32), k_oth[:, half:].astype(f32))
    halo = halo_ref[...].astype(f32)
    before = jnp.where(first, halo, near)
    after = jnp.where(first, near, halo)
    plane = rows * cols
    lane = lax.broadcasted_iota(jnp.int32, (1, 1, cols), 2)
    faces = [0.25 * lax.shift_left(1, face_ref[f]).astype(f32) for f in range(6)]
    w_s[6] = ((faces[0] + faces[1]) + (faces[2] + faces[3])) + (faces[4] + faces[5])
    faces[4] = jnp.where(lane == 0, 0.0, faces[4])
    faces[5] = jnp.where(lane == cols - 1, 0.0, faces[5])
    for f in range(6):
        w_s[f] = faces[f]
    k_s[...] = k_ref[...].astype(f32)
    for x in range(2):
        for y in range(rows):
            at = (x * rows + y) * cols
            mid = k_s[:, at : at + cols]
            w = [w_s[f, x, y : y + 1, :] for f in range(7)]
            down = before[:, y * cols : (y + 1) * cols] if x == 0 else k_s[:, at - plane : at - plane + cols]
            up = after[:, y * cols : (y + 1) * cols] if x == 1 else k_s[:, at + plane : at + plane + cols]
            out = w[0] * down + w[1] * up - w[6] * mid
            if y > 0:
                out += w[2] * k_s[:, at - cols : at]
            if y < rows - 1:
                out += w[3] * k_s[:, at + cols : at + 2 * cols]
            out += w[4] * pltpu.roll(mid, 1, 1)
            out += w[5] * pltpu.roll(mid, cols - 1, 1)
            base_s[:, at : at + cols] = mid + step_size * out
            lap_s[:, at : at + cols] = out.astype(bf16)
    base_ref[...] = base_s[pl.ds(pl.multiple_of(c_ref[1] * base_ref.shape[0], 8), base_ref.shape[0]), :]
    m_ref[...] = dot(u_ref[...], lap_s[...], 1, 1)


def sweep(kt_ref, u_ref, v_ref, g_ref, ov_ref, start, stop, store, tile=512):
    block = stop - start

    def turn(i, _):
        at = pl.multiple_of(start + i * block, block)
        v = v_ref[:, pl.ds(at, block)]
        g = g_ref[:, pl.ds(at, block)]
        acc = None
        for row in range(0, u_ref.shape[1], tile):
            field = dot(kt_ref[row : row + tile, :], v, 1, 0)
            react = (field * (g - field * field)).astype(bf16)
            ov_ref[row : row + tile, :] += dot(react, v, 1, 1)
            part = dot(u_ref[:, row : row + tile], react, 1, 0)
            acc = part if acc is None else acc + part
        store(pl.ds(pl.multiple_of(at - start, block), block), acc)
        return 0

    lax.fori_loop(0, (stop - start) // block, turn, 0)


def part_body(start, has_old, back, kt_ref, u_ref, v_ref, g_ref, *refs):
    refs = list(refs)
    old_ref = refs.pop(0) if has_old & 1 else None
    far_ref = refs.pop(0) if has_old & 2 else None
    l_ref, ov_ref = refs[:2]
    ov_s = refs[2] if back else ov_ref
    ov_s[...] = jnp.zeros_like(ov_s) if far_ref is None else far_ref[...]

    done = 0 if old_ref is None else old_ref.shape[1]

    def store(here, acc):
        if done:
            l_ref[:, :done] = old_ref[...] + acc[:, :done]
            l_ref[:, done:] = acc[:, done:]
        else:
            l_ref[:, here] = acc

    sweep(kt_ref, u_ref, v_ref, g_ref, ov_s, start, start + l_ref.shape[1], store)
    if back:
        ov_ref[...] = ov_s[...].T.astype(bf16)


def last_body(
    scale, at_ref, kt_ref, u_ref, v_ref, g_ref, l_ref, more_ref, ov_ref, got_ref, ma_ref, mb_ref, core_ref,
    out_ref, me_ref, up_ref, dn_ref, away_ref, ov_s, tot_s, w_s,
):
    rank, count = out_ref.shape
    middle = count - count // 2
    start = middle + more_ref.shape[1]
    ov_s[...] = ov_ref[...]
    w = core_ref[...].astype(bf16).astype(f32) * 0.125 + scale * (ma_ref[...] + mb_ref[...])
    high = w.astype(bf16)
    w_s[:rank, :] = high
    w_s[rank:, :] = (w - high.astype(f32)).astype(bf16)

    def send(at, size, total):
        side = dot(w_s[...], v_ref[:, at : at + size], 1, 0)
        out_ref[:, at : at + size] = (scale * total + (side[:rank] + side[rank:])).astype(bf16)

    send(0, middle, l_ref[:, :middle])
    send(middle, start - middle, l_ref[:, middle:start] + more_ref[...])

    def store(here, acc):
        send(start, count - start, l_ref[:, start:] + acc)

    sweep(kt_ref, u_ref, v_ref, g_ref, ov_s, start, count, store)
    tot_s[...] = ov_s[...].T + got_ref[...].astype(f32)
    rows = me_ref.shape[0]
    y = at_ref[2]

    def part(turn):
        return tot_s[pl.ds(pl.multiple_of(((y + turn) % 4) * rows, rows), rows), :]

    me_ref[...] = part(0)
    up_ref[...] = part(1).astype(bf16)
    away_ref[...] = part(2).astype(bf16)
    dn_ref[...] = part(3).astype(bf16)


def done_body(scale, base_ref, mine_ref, got_ref, out_ref):
    _, depth, rows, cols = out_ref.shape
    new = base_ref[...] + scale * (mine_ref[...] + got_ref[...].astype(f32))
    for x in range(depth):
        for y in range(rows):
            at = (x * rows + y) * cols
            out_ref[:, x, y, :] = new[:, at : at + cols]


def pair_body(at_ref, me_ref, rc_ref, rd_ref, re_ref, mine_ref, send_ref, tot_s):
    rows = mine_ref.shape[0]
    tot_s[...] = (me_ref[...] + rc_ref[...].astype(f32)) + (rd_ref[...].astype(f32) + re_ref[...].astype(f32))
    xh = at_ref[3]
    mine_ref[...] = tot_s[pl.ds(pl.multiple_of(xh * rows, rows), rows), :]
    send_ref[...] = tot_s[pl.ds(pl.multiple_of((1 - xh) * rows, rows), rows), :].astype(bf16)


def ring(n, k):
    return [(i, (i + k) % n) for i in range(n)]


def per_device(basis_u, basis_v, core_s, face_class, sample_class):
    narrow, depth_x, rows_y, cols_z = basis_u.shape
    rank = core_s.shape[0]
    n_samp, n_space = 8, 16
    cells = depth_x * rows_y * cols_z
    lanes, samp_rows = basis_v.shape
    half = samp_rows // 2
    cell_weight = rank / (cells * n_space)
    samp_weight = rank / (samp_rows * n_samp)
    core_at = lax.axis_index("c")
    where_at = jnp.stack([core_at, lax.axis_index(SAMP), lax.axis_index("y"), lax.axis_index("xh")]).astype(jnp.int32)
    swap = ring(2, 1)

    (v_wide,) = small(fan_body, [basis_v], [((n_space // 2, 2, lanes, half), bf16, False)])
    v = resident(lax.all_to_all(v_wide.reshape(rank, half), SPACE, 0, 0, tiled=True))
    u1 = resident(lax.ppermute(basis_u, "xh", swap))
    (pair,) = small(flat_body, [basis_u, u1], [((2 * narrow, cells), bf16, True)], [(basis_u.shape, f32)])
    around = [resident(lax.ppermute(pair, "y", ring(4, k))) for k in (1, 3, 2)]
    u_own, k_own, kt_own, edge = small(
        prep_body,
        [pair, *around, core_s],
        [((rank, cells), bf16, True), ((rank, cells), bf16, True), ((cells, rank), bf16, True), ((rank, cells // 2), bf16, True)],
        at=where_at,
    )
    u_oth = resident(lax.ppermute(u_own, "c", swap))
    chips = n_space // 2
    hops = [(2 * i + 1, 2 * i + 2) for i in range(chips - 1)] + [(2 * i + 2, 2 * i + 1) for i in range(chips - 1)]
    halo = resident(lax.ppermute(edge, SPACE, hops))

    growth = 0.5 + 0.5 * lax.dynamic_slice_in_dim(sample_class, core_at * half, half, 0).astype(f32)
    growth = resident(growth.reshape(1, half))
    scale = step_size * cell_weight
    quart = half // 2
    main = lambda start, kinds, back: functools.partial(part_body, start, kinds, back)
    l_first, ov_first = small(
        main(0, 0, False), [kt_own, u_own, v, growth], [((rank, quart), f32, True), ((cells, rank), f32, True)]
    )
    kt_oth, base, m_own = small(
        functools.partial(mid_body, rows_y, cols_z),
        [u_oth, core_s, k_own, halo, face_class, u_own],
        [((cells, rank), bf16, True), ((narrow, cells), f32, False), ((rank, rank), f32, True)],
        [((rank, cells), f32), ((rank, cells), bf16), ((7,) + face_class.shape[1:], f32), ((rank, cells), f32)],
        at=where_at,
        held=(ov_first, kt_own, l_first),
    )
    m_oth = resident(lax.ppermute(m_own, "c", swap))
    l_most, ov_send = small(
        main(0, 1, True),
        [kt_oth, u_oth, v, growth, l_first],
        [((rank, half), f32, True), ((rank, cells), bf16, True)],
        [((cells, rank), f32)],
        held=(ov_first, kt_own, u_own),
    )
    got = resident(lax.ppermute(ov_send, "c", swap))
    l_more, ov_more = small(
        main(quart, 2, False),
        [kt_own, u_own, v, growth, ov_first],
        [((rank, quart // 2), f32, True), ((cells, rank), f32, True)],
        held=(l_most, ov_send),
    )
    rows = rank // 4
    l_part, me, up, dn, away = small(
        functools.partial(last_body, scale),
        [kt_own, u_own, v, growth, l_most, l_more, ov_more, got, m_own, m_oth, core_s],
        [((rank, half), bf16, False), ((rows, cells), f32, True)] + [((rows, cells), bf16, True)] * 3,
        [((cells, rank), f32), ((rank, cells), f32), ((2 * rank, rank), bf16)],
        at=where_at,
    )

    l_got = lax.all_to_all(l_part, SPACE, 0, 0, tiled=True)
    l_new = l_got.reshape(n_space // 2, 2, lanes, half).astype(f32).sum(0)
    l_new = jnp.transpose(l_new, (1, 0, 2)).reshape(lanes, samp_rows)

    near = []
    for part, k in ((up, 1), (dn, 3), (away, 2)):
        near.append(resident(lax.ppermute(part, "y", ring(4, k))))
    mine, send = small(
        pair_body,
        [me, *near],
        [((narrow, cells), f32, True), ((narrow, cells), bf16, True)],
        [((rows, cells), f32)],
        at=where_at,
    )
    (k_new,) = small(
        functools.partial(done_body, step_size * samp_weight),
        [base, mine, resident(lax.ppermute(send, "xh", swap))],
        [(basis_u.shape, f32, False)],
    )
    return (k_new, l_new)


def solution(mesh):
    fine = Mesh(mesh.devices.reshape(4, 2, 2, 4, 2), SPACE + SAMP)
    return jax.shard_map(
        per_device,
        mesh=fine,
        in_specs=(P(SAMP, SPACE, None, None), P(SPACE, SAMP), P(), P(None, SPACE, None, None), P(SAMP)),
        out_specs=(P(SAMP, SPACE, None, None), P(SPACE, SAMP)),
        check_vma=False,
    )
```

```python
import functools

import jax
import jax.numpy as jnp
from jax import lax
from jax.experimental import pallas as pl
from jax.experimental.pallas import tpu as pltpu
from jax.sharding import Mesh, PartitionSpec as P

step_size = 0.1
SPACE = ("z", "xl", "c")
SAMP = ("y", "xh")
bf16, f32 = jnp.bfloat16, jnp.float32


def dot(a, b, ca, cb):
    return lax.dot_general(a, b, (((ca,), (cb,)), ((), ())), preferred_element_type=f32)


def resident(x):
    return pltpu.with_memory_space_constraint(x, pltpu.MemorySpace.VMEM)


def small(body, args, outs, scratch=(), at=None, held=(), limit=24):
    vm = pl.BlockSpec(memory_space=pltpu.VMEM)
    scalars = [] if at is None else [at]
    n_read = len(scalars) + len(args)

    def reading(*refs):
        body(*refs[:n_read], *refs[n_read + len(held) :])

    return pl.pallas_call(
        reading,
        in_specs=[pl.BlockSpec(memory_space=pltpu.SMEM)] * len(scalars)
        + [vm] * (len(args) + len(held)),
        out_specs=[pl.BlockSpec(memory_space=pl.ANY) if keep is None else vm for _, _, keep in outs],
        out_shape=[(pltpu.VMEM if keep else pltpu.HBM)(shape, dtype) for shape, dtype, keep in outs],
        scratch_shapes=[pltpu.VMEM(*kind) if isinstance(kind, tuple) else kind for kind in scratch],
        compiler_params=pltpu.CompilerParams(vmem_limit_bytes=limit << 20),
    )(*scalars, *args, *held)


def fan_body(v_ref, out_ref):
    half = out_ref.shape[-1]
    for k in range(out_ref.shape[0]):
        out_ref[k, 0] = v_ref[:, :half]
        out_ref[k, 1] = v_ref[:, half:]


def flat_body(own_ref, got_ref, out_ref, u_s):
    narrow, depth, rows, cols = own_ref.shape
    for i, ref in enumerate((own_ref, got_ref)):
        u_s[...] = ref[...].astype(f32)
        for x in range(depth):
            for y in range(rows):
                at = (x * rows + y) * cols
                out_ref[i * narrow : (i + 1) * narrow, at : at + cols] = u_s[:, x, y, :].astype(bf16)


def prep_body(at_ref, u_ref, a_ref, b_ref, c_ref, core_ref, full_ref, k_ref, kt_ref, halo_ref):
    narrow, cells = u_ref.shape[0] // 2, u_ref.shape[1]
    half = cells // 2
    y, xh = at_ref[2], at_ref[3]

    def put(turn, flip, value):
        row = (((y + turn) % 4) * 2 + (xh if flip == 0 else 1 - xh)) * narrow
        full_ref[pl.ds(pl.multiple_of(row, narrow), narrow), :] = value

    for turn, ref in ((0, u_ref), (3, a_ref), (1, b_ref), (2, c_ref)):
        put(turn, 0, ref[:narrow, :])
        put(turn, 1, ref[narrow:, :])
    k_own = dot(core_ref[...].astype(bf16), full_ref[...], 0, 0).astype(bf16)
    k_ref[...] = k_own
    kt_ref[...] = k_own.T
    first = at_ref[0] == 0

    @pl.when(first)
    def _():
        halo_ref[...] = k_own[:, :half]

    @pl.when(jnp.logical_not(first))
    def _():
        halo_ref[...] = k_own[:, half:]


def mid_body(rows, cols, c_ref, oth_ref, core_ref, k_ref, halo_ref, face_ref, u_ref, kt_ref, base_ref, m_ref, base_s, lap_s, w_s, k_s):
    half = oth_ref.shape[1] // 2
    k_oth = dot(core_ref[...].astype(bf16), oth_ref[...], 0, 0).astype(bf16)
    kt_ref[...] = k_oth.T
    first = c_ref[0] == 0
    near = jnp.where(first, k_oth[:, :half].astype(f32), k_oth[:, half:].astype(f32))
    halo = halo_ref[...].astype(f32)
    before = jnp.where(first, halo, near)
    after = jnp.where(first, near, halo)
    plane = rows * cols
    lane = lax.broadcasted_iota(jnp.int32, (1, 1, cols), 2)
    faces = [0.25 * lax.shift_left(1, face_ref[f]).astype(f32) for f in range(6)]
    w_s[6] = ((faces[0] + faces[1]) + (faces[2] + faces[3])) + (faces[4] + faces[5])
    faces[4] = jnp.where(lane == 0, 0.0, faces[4])
    faces[5] = jnp.where(lane == cols - 1, 0.0, faces[5])
    for f in range(6):
        w_s[f] = faces[f]
    k_s[...] = k_ref[...].astype(f32)
    for x in range(2):
        for y in range(rows):
            at = (x * rows + y) * cols
            mid = k_s[:, at : at + cols]
            w = [w_s[f, x, y : y + 1, :] for f in range(7)]
            down = before[:, y * cols : (y + 1) * cols] if x == 0 else k_s[:, at - plane : at - plane + cols]
            up = after[:, y * cols : (y + 1) * cols] if x == 1 else k_s[:, at + plane : at + plane + cols]
            out = w[0] * down + w[1] * up - w[6] * mid
            if y > 0:
                out += w[2] * k_s[:, at - cols : at]
            if y < rows - 1:
                out += w[3] * k_s[:, at + cols : at + 2 * cols]
            out += w[4] * pltpu.roll(mid, 1, 1)
            out += w[5] * pltpu.roll(mid, cols - 1, 1)
            base_s[:, at : at + cols] = mid + step_size * out
            lap_s[:, at : at + cols] = out.astype(bf16)
    base_ref[...] = base_s[pl.ds(pl.multiple_of(c_ref[1] * base_ref.shape[0], 8), base_ref.shape[0]), :]
    m_ref[...] = dot(u_ref[...], lap_s[...], 1, 1)


def sweep(kt_ref, u_ref, v_ref, g_ref, ov_ref, start, stop, store, tile=512):
    block = stop - start

    def turn(i, _):
        at = pl.multiple_of(start + i * block, block)
        v = v_ref[:, pl.ds(at, block)]
        g = g_ref[:, pl.ds(at, block)]
        acc = None
        for row in range(0, u_ref.shape[1], tile):
            field = dot(kt_ref[row : row + tile, :], v, 1, 0)
            react = (field * (g - field * field)).astype(bf16)
            ov_ref[row : row + tile, :] += dot(react, v, 1, 1)
            part = dot(u_ref[:, row : row + tile], react, 1, 0)
            acc = part if acc is None else acc + part
        store(pl.ds(pl.multiple_of(at - start, block), block), acc)
        return 0

    lax.fori_loop(0, (stop - start) // block, turn, 0)


def part_body(start, has_old, back, kt_ref, u_ref, v_ref, g_ref, *refs):
    refs = list(refs)
    old_ref = refs.pop(0) if has_old & 1 else None
    far_ref = refs.pop(0) if has_old & 2 else None
    l_ref, ov_ref = refs[:2]
    ov_s = refs[2] if back else ov_ref
    ov_s[...] = jnp.zeros_like(ov_s) if far_ref is None else far_ref[...]

    done = 0 if old_ref is None else old_ref.shape[1]

    def store(here, acc):
        if done:
            l_ref[:, :done] = old_ref[...] + acc[:, :done]
            l_ref[:, done:] = acc[:, done:]
        else:
            l_ref[:, here] = acc

    sweep(kt_ref, u_ref, v_ref, g_ref, ov_s, start, start + l_ref.shape[1], store)
    if back:
        ov_ref[...] = ov_s[...].T.astype(bf16)


def last_body(
    scale, at_ref, kt_ref, u_ref, v_ref, g_ref, l_ref, more_ref, ov_ref, got_ref, ma_ref, mb_ref, core_ref,
    out_hbm, me_ref, up_ref, dn_ref, away_ref, ov_s, tot_s, w_s, out_ref, sems,
):
    rank, count = out_ref.shape
    middle = count - count // 2
    start = middle + more_ref.shape[1]
    ov_s[...] = ov_ref[...]
    w = core_ref[...].astype(bf16).astype(f32) * 0.125 + scale * (ma_ref[...] + mb_ref[...])
    high = w.astype(bf16)
    w_s[:rank, :] = high
    w_s[rank:, :] = (w - high.astype(f32)).astype(bf16)

    def send(at, size, total):
        side = dot(w_s[...], v_ref[:, at : at + size], 1, 0)
        out_ref[:, at : at + size] = (scale * total + (side[:rank] + side[rank:])).astype(bf16)

    send(0, middle, l_ref[:, :middle])
    send(middle, start - middle, l_ref[:, middle:start] + more_ref[...])
    leave = [
        pltpu.make_async_copy(out_ref.at[:, :start], out_hbm.at[:, :start], sems.at[0]),
        pltpu.make_async_copy(out_ref.at[:, start:], out_hbm.at[:, start:], sems.at[1]),
    ]
    leave[0].start()

    def store(here, acc):
        send(start, count - start, l_ref[:, start:] + acc)

    sweep(kt_ref, u_ref, v_ref, g_ref, ov_s, start, count, store)
    leave[1].start()
    tot_s[...] = ov_s[...].T + got_ref[...].astype(f32)
    rows = me_ref.shape[0]
    y = at_ref[2]

    def part(turn):
        return tot_s[pl.ds(pl.multiple_of(((y + turn) % 4) * rows, rows), rows), :]

    me_ref[...] = part(0)
    up_ref[...] = part(1).astype(bf16)
    away_ref[...] = part(2).astype(bf16)
    dn_ref[...] = part(3).astype(bf16)
    for copy in leave:
        copy.wait()


def gain_body(got_ref, out_ref):
    chips, parts, _, half = got_ref.shape
    for p in range(parts):
        total = got_ref[0, p].astype(f32)
        for k in range(1, chips):
            total = total + got_ref[k, p].astype(f32)
        out_ref[:, p * half : (p + 1) * half] = total


def done_body(scale, base_ref, mine_ref, got_ref, out_ref):
    _, depth, rows, cols = out_ref.shape
    new = base_ref[...] + scale * (mine_ref[...] + got_ref[...].astype(f32))
    for x in range(depth):
        for y in range(rows):
            at = (x * rows + y) * cols
            out_ref[:, x, y, :] = new[:, at : at + cols]


def pair_body(at_ref, me_ref, rc_ref, rd_ref, re_ref, mine_ref, send_ref, tot_s):
    rows = mine_ref.shape[0]
    tot_s[...] = (me_ref[...] + rc_ref[...].astype(f32)) + (rd_ref[...].astype(f32) + re_ref[...].astype(f32))
    xh = at_ref[3]
    mine_ref[...] = tot_s[pl.ds(pl.multiple_of(xh * rows, rows), rows), :]
    send_ref[...] = tot_s[pl.ds(pl.multiple_of((1 - xh) * rows, rows), rows), :].astype(bf16)


def ring(n, k):
    return [(i, (i + k) % n) for i in range(n)]


def per_device(basis_u, basis_v, core_s, face_class, sample_class):
    narrow, depth_x, rows_y, cols_z = basis_u.shape
    rank = core_s.shape[0]
    n_samp, n_space = 8, 16
    cells = depth_x * rows_y * cols_z
    lanes, samp_rows = basis_v.shape
    half = samp_rows // 2
    cell_weight = rank / (cells * n_space)
    samp_weight = rank / (samp_rows * n_samp)
    core_at = lax.axis_index("c")
    where_at = jnp.stack([core_at, lax.axis_index(SAMP), lax.axis_index("y"), lax.axis_index("xh")]).astype(jnp.int32)
    swap = ring(2, 1)

    (v_wide,) = small(fan_body, [basis_v], [((n_space // 2, 2, lanes, half), bf16, False)])
    v = resident(lax.all_to_all(v_wide.reshape(rank, half), SPACE, 0, 0, tiled=True))
    u1 = resident(lax.ppermute(basis_u, "xh", swap))
    (pair,) = small(flat_body, [basis_u, u1], [((2 * narrow, cells), bf16, True)], [(basis_u.shape, f32)])
    around = [resident(lax.ppermute(pair, "y", ring(4, k))) for k in (1, 3, 2)]
    u_own, k_own, kt_own, edge = small(
        prep_body,
        [pair, *around, core_s],
        [((rank, cells), bf16, True), ((rank, cells), bf16, True), ((cells, rank), bf16, True), ((rank, cells // 2), bf16, True)],
        at=where_at,
    )
    u_oth = resident(lax.ppermute(u_own, "c", swap))
    chips = n_space // 2
    hops = [(2 * i + 1, 2 * i + 2) for i in range(chips - 1)] + [(2 * i + 2, 2 * i + 1) for i in range(chips - 1)]
    halo = resident(lax.ppermute(edge, SPACE, hops))

    growth = 0.5 + 0.5 * lax.dynamic_slice_in_dim(sample_class, core_at * half, half, 0).astype(f32)
    growth = resident(growth.reshape(1, half))
    scale = step_size * cell_weight
    quart = half // 2
    main = lambda start, kinds, back: functools.partial(part_body, start, kinds, back)
    l_first, ov_first = small(
        main(0, 0, False), [kt_own, u_own, v, growth], [((rank, quart), f32, True), ((cells, rank), f32, True)]
    )
    kt_oth, base, m_own = small(
        functools.partial(mid_body, rows_y, cols_z),
        [u_oth, core_s, k_own, halo, face_class, u_own],
        [((cells, rank), bf16, True), ((narrow, cells), f32, False), ((rank, rank), f32, True)],
        [((rank, cells), f32), ((rank, cells), bf16), ((7,) + face_class.shape[1:], f32), ((rank, cells), f32)],
        at=where_at,
        held=(ov_first, kt_own, l_first),
    )
    m_oth = resident(lax.ppermute(m_own, "c", swap))
    l_most, ov_send = small(
        main(0, 1, True),
        [kt_oth, u_oth, v, growth, l_first],
        [((rank, half), f32, True), ((rank, cells), bf16, True)],
        [((cells, rank), f32)],
        held=(ov_first, kt_own, u_own),
    )
    got = resident(lax.ppermute(ov_send, "c", swap))
    l_more, ov_more = small(
        main(quart, 2, False),
        [kt_own, u_own, v, growth, ov_first],
        [((rank, quart // 2), f32, True), ((cells, rank), f32, True)],
        held=(l_most, ov_send),
    )
    rows = rank // 4
    l_part, me, up, dn, away = small(
        functools.partial(last_body, scale),
        [kt_own, u_own, v, growth, l_most, l_more, ov_more, got, m_own, m_oth, core_s],
        [((rank, half), bf16, None), ((rows, cells), f32, True)] + [((rows, cells), bf16, True)] * 3,
        [
            ((cells, rank), f32),
            ((rank, cells), f32),
            ((2 * rank, rank), bf16),
            ((rank, half), bf16),
            pltpu.SemaphoreType.DMA((2,)),
        ],
        at=where_at,
    )

    l_got = lax.all_to_all(l_part, SPACE, 0, 0, tiled=True)
    (l_new,) = small(
        gain_body, [resident(l_got.reshape(n_space // 2, 2, lanes, half))], [((lanes, samp_rows), f32, False)]
    )

    near = []
    for part, k in ((up, 1), (dn, 3), (away, 2)):
        near.append(resident(lax.ppermute(part, "y", ring(4, k))))
    mine, send = small(
        pair_body,
        [me, *near],
        [((narrow, cells), f32, True), ((narrow, cells), bf16, True)],
        [((rows, cells), f32)],
        at=where_at,
    )
    last = resident(lax.ppermute(send, "xh", swap))
    (k_new,) = small(
        functools.partial(done_body, step_size * samp_weight),
        [base, mine, last],
        [(basis_u.shape, f32, False)],
    )
    return (k_new, l_new)


def solution(mesh):
    fine = Mesh(mesh.devices.reshape(4, 2, 2, 4, 2), SPACE + SAMP)
    return jax.shard_map(
        per_device,
        mesh=fine,
        in_specs=(P(SAMP, SPACE, None, None), P(SPACE, SAMP), P(), P(None, SPACE, None, None), P(SAMP)),
        out_specs=(P(SAMP, SPACE, None, None), P(SPACE, SAMP)),
        check_vma=False,
    )
```

```python
import functools

import jax
import jax.numpy as jnp
from jax import lax
from jax.experimental import pallas as pl
from jax.experimental.pallas import tpu as pltpu
from jax.sharding import Mesh, PartitionSpec as P

step_size = 0.1
SPACE = ("z", "xl", "c")
SAMP = ("y", "xh")
bf16, f32 = jnp.bfloat16, jnp.float32


def dot(a, b, ca, cb):
    return lax.dot_general(a, b, (((ca,), (cb,)), ((), ())), preferred_element_type=f32)


def resident(x):
    return pltpu.with_memory_space_constraint(x, pltpu.MemorySpace.VMEM)


def small(body, args, outs, scratch=(), at=None, held=(), limit=24):
    vm = pl.BlockSpec(memory_space=pltpu.VMEM)
    scalars = [] if at is None else [at]
    n_read = len(scalars) + len(args)

    def reading(*refs):
        body(*refs[:n_read], *refs[n_read + len(held) :])

    return pl.pallas_call(
        reading,
        in_specs=[pl.BlockSpec(memory_space=pltpu.SMEM)] * len(scalars)
        + [vm] * (len(args) + len(held)),
        out_specs=[pl.BlockSpec(memory_space=pl.ANY) if keep is None else vm for _, _, keep in outs],
        out_shape=[(pltpu.VMEM if keep else pltpu.HBM)(shape, dtype) for shape, dtype, keep in outs],
        scratch_shapes=[pltpu.VMEM(*kind) if isinstance(kind, tuple) else kind for kind in scratch],
        compiler_params=pltpu.CompilerParams(vmem_limit_bytes=limit << 20),
    )(*scalars, *args, *held)


def fan_body(v_ref, out_ref):
    half = out_ref.shape[-1]
    for k in range(out_ref.shape[0]):
        out_ref[k, 0] = v_ref[:, :half]
        out_ref[k, 1] = v_ref[:, half:]


def flat_body(own_ref, got_ref, out_ref, u_s):
    narrow, depth, rows, cols = own_ref.shape
    for i, ref in enumerate((own_ref, got_ref)):
        u_s[...] = ref[...].astype(f32)
        for x in range(depth):
            for y in range(rows):
                at = (x * rows + y) * cols
                out_ref[i * narrow : (i + 1) * narrow, at : at + cols] = u_s[:, x, y, :].astype(bf16)


def prep_body(at_ref, u_ref, a_ref, b_ref, c_ref, core_ref, full_ref, k_ref, kt_ref, halo_ref):
    narrow, cells = u_ref.shape[0] // 2, u_ref.shape[1]
    half = cells // 2
    y, xh = at_ref[2], at_ref[3]

    def put(turn, flip, value):
        row = (((y + turn) % 4) * 2 + (xh if flip == 0 else 1 - xh)) * narrow
        full_ref[pl.ds(pl.multiple_of(row, narrow), narrow), :] = value

    for turn, ref in ((0, u_ref), (3, a_ref), (1, b_ref), (2, c_ref)):
        put(turn, 0, ref[:narrow, :])
        put(turn, 1, ref[narrow:, :])
    k_own = dot(core_ref[...].astype(bf16), full_ref[...], 0, 0).astype(bf16)
    k_ref[...] = k_own
    kt_ref[...] = k_own.T
    first = at_ref[0] == 0

    @pl.when(first)
    def _():
        halo_ref[...] = k_own[:, :half]

    @pl.when(jnp.logical_not(first))
    def _():
        halo_ref[...] = k_own[:, half:]


def mid_body(rows, cols, c_ref, oth_ref, core_ref, k_ref, halo_ref, face_ref, u_ref, kt_ref, base_ref, m_ref, base_s, lap_s, w_s, k_s):
    half = oth_ref.shape[1] // 2
    k_oth = dot(core_ref[...].astype(bf16), oth_ref[...], 0, 0).astype(bf16)
    kt_ref[...] = k_oth.T
    first = c_ref[0] == 0
    near = jnp.where(first, k_oth[:, :half].astype(f32), k_oth[:, half:].astype(f32))
    halo = halo_ref[...].astype(f32)
    before = jnp.where(first, halo, near)
    after = jnp.where(first, near, halo)
    plane = rows * cols
    lane = lax.broadcasted_iota(jnp.int32, (1, 1, cols), 2)
    faces = [0.25 * lax.shift_left(1, face_ref[f]).astype(f32) for f in range(6)]
    w_s[6] = ((faces[0] + faces[1]) + (faces[2] + faces[3])) + (faces[4] + faces[5])
    faces[4] = jnp.where(lane == 0, 0.0, faces[4])
    faces[5] = jnp.where(lane == cols - 1, 0.0, faces[5])
    for f in range(6):
        w_s[f] = faces[f]
    k_s[...] = k_ref[...].astype(f32)
    for x in range(2):
        for y in range(rows):
            at = (x * rows + y) * cols
            mid = k_s[:, at : at + cols]
            w = [w_s[f, x, y : y + 1, :] for f in range(7)]
            down = before[:, y * cols : (y + 1) * cols] if x == 0 else k_s[:, at - plane : at - plane + cols]
            up = after[:, y * cols : (y + 1) * cols] if x == 1 else k_s[:, at + plane : at + plane + cols]
            out = w[0] * down + w[1] * up - w[6] * mid
            if y > 0:
                out += w[2] * k_s[:, at - cols : at]
            if y < rows - 1:
                out += w[3] * k_s[:, at + cols : at + 2 * cols]
            out += w[4] * pltpu.roll(mid, 1, 1)
            out += w[5] * pltpu.roll(mid, cols - 1, 1)
            base_s[:, at : at + cols] = mid + step_size * out
            lap_s[:, at : at + cols] = out.astype(bf16)
    base_ref[...] = base_s[pl.ds(pl.multiple_of(c_ref[1] * base_ref.shape[0], 8), base_ref.shape[0]), :]
    m_ref[...] = dot(u_ref[...], lap_s[...], 1, 1)


def sweep(kt_ref, u_ref, v_ref, g_ref, was_ref, ov_ref, start, stop, store, tile=512):
    block = stop - start

    def turn(i, _):
        at = pl.multiple_of(start + i * block, block)
        v = v_ref[:, pl.ds(at, block)]
        g = g_ref[:, pl.ds(at, block)]
        acc = None
        for row in range(0, u_ref.shape[1], tile):
            field = dot(kt_ref[row : row + tile, :], v, 1, 0)
            react = (field * (g - field * field)).astype(bf16)
            onto = dot(react, v, 1, 1)
            ov_ref[row : row + tile, :] = onto if was_ref is None else was_ref[row : row + tile, :] + onto
            part = dot(u_ref[:, row : row + tile], react, 1, 0)
            acc = part if acc is None else acc + part
        store(pl.ds(pl.multiple_of(at - start, block), block), acc)
        return 0

    lax.fori_loop(0, (stop - start) // block, turn, 0)


def part_body(start, has_old, back, kt_ref, u_ref, v_ref, g_ref, *refs):
    refs = list(refs)
    old_ref = refs.pop(0) if has_old & 1 else None
    far_ref = refs.pop(0) if has_old & 2 else None
    l_ref, ov_ref = refs[:2]
    ov_s = refs[2] if back else ov_ref

    done = 0 if old_ref is None else old_ref.shape[1]

    def store(here, acc):
        if done:
            l_ref[:, :done] = old_ref[...] + acc[:, :done]
            l_ref[:, done:] = acc[:, done:]
        else:
            l_ref[:, here] = acc

    sweep(kt_ref, u_ref, v_ref, g_ref, far_ref, ov_s, start, start + l_ref.shape[1], store)
    if back:
        ov_ref[...] = ov_s[...].T.astype(bf16)


def last_body(
    scale, at_ref, kt_ref, u_ref, v_ref, g_ref, l_ref, more_ref, ov_ref, got_ref, ma_ref, mb_ref, core_ref,
    out_hbm, me_ref, up_ref, dn_ref, away_ref, ov_s, tot_s, w_s, out_ref, sems,
):
    rank, count = out_ref.shape
    middle = count - count // 2
    start = middle + more_ref.shape[1]
    w = core_ref[...].astype(bf16).astype(f32) * 0.125 + scale * (ma_ref[...] + mb_ref[...])
    high = w.astype(bf16)
    w_s[:rank, :] = high
    w_s[rank:, :] = (w - high.astype(f32)).astype(bf16)

    def send(at, size, total):
        side = dot(w_s[...], v_ref[:, at : at + size], 1, 0)
        out_ref[:, at : at + size] = (scale * total + (side[:rank] + side[rank:])).astype(bf16)

    send(0, middle, l_ref[:, :middle])
    send(middle, start - middle, l_ref[:, middle:start] + more_ref[...])
    leave = [
        pltpu.make_async_copy(out_ref.at[:, :start], out_hbm.at[:, :start], sems.at[0]),
        pltpu.make_async_copy(out_ref.at[:, start:], out_hbm.at[:, start:], sems.at[1]),
    ]
    leave[0].start()

    def store(here, acc):
        send(start, count - start, l_ref[:, start:] + acc)

    sweep(kt_ref, u_ref, v_ref, g_ref, ov_ref, ov_s, start, count, store)
    leave[1].start()
    tot_s[...] = ov_s[...].T + got_ref[...].astype(f32)
    rows = me_ref.shape[0]
    y = at_ref[2]

    def part(turn):
        return tot_s[pl.ds(pl.multiple_of(((y + turn) % 4) * rows, rows), rows), :]

    me_ref[...] = part(0)
    up_ref[...] = part(1).astype(bf16)
    away_ref[...] = part(2).astype(bf16)
    dn_ref[...] = part(3).astype(bf16)
    for copy in leave:
        copy.wait()


def gain_body(got_ref, out_ref):
    chips, parts, _, half = got_ref.shape
    for p in range(parts):
        total = got_ref[0, p].astype(f32)
        for k in range(1, chips):
            total = total + got_ref[k, p].astype(f32)
        out_ref[:, p * half : (p + 1) * half] = total


def done_body(scale, base_ref, mine_ref, got_ref, out_ref):
    _, depth, rows, cols = out_ref.shape
    new = base_ref[...] + scale * (mine_ref[...] + got_ref[...].astype(f32))
    for x in range(depth):
        for y in range(rows):
            at = (x * rows + y) * cols
            out_ref[:, x, y, :] = new[:, at : at + cols]


def pair_body(at_ref, me_ref, rc_ref, rd_ref, re_ref, mine_ref, send_ref, tot_s):
    rows = mine_ref.shape[0]
    tot_s[...] = (me_ref[...] + rc_ref[...].astype(f32)) + (rd_ref[...].astype(f32) + re_ref[...].astype(f32))
    xh = at_ref[3]
    mine_ref[...] = tot_s[pl.ds(pl.multiple_of(xh * rows, rows), rows), :]
    send_ref[...] = tot_s[pl.ds(pl.multiple_of((1 - xh) * rows, rows), rows), :].astype(bf16)


def ring(n, k):
    return [(i, (i + k) % n) for i in range(n)]


def per_device(basis_u, basis_v, core_s, face_class, sample_class):
    narrow, depth_x, rows_y, cols_z = basis_u.shape
    rank = core_s.shape[0]
    n_samp, n_space = 8, 16
    cells = depth_x * rows_y * cols_z
    lanes, samp_rows = basis_v.shape
    half = samp_rows // 2
    cell_weight = rank / (cells * n_space)
    samp_weight = rank / (samp_rows * n_samp)
    core_at = lax.axis_index("c")
    where_at = jnp.stack([core_at, lax.axis_index(SAMP), lax.axis_index("y"), lax.axis_index("xh")]).astype(jnp.int32)
    swap = ring(2, 1)

    (v_wide,) = small(fan_body, [basis_v], [((n_space // 2, 2, lanes, half), bf16, False)])
    v = resident(lax.all_to_all(v_wide.reshape(rank, half), SPACE, 0, 0, tiled=True))
    u1 = resident(lax.ppermute(basis_u, "xh", swap))
    (pair,) = small(flat_body, [basis_u, u1], [((2 * narrow, cells), bf16, True)], [(basis_u.shape, f32)])
    around = [resident(lax.ppermute(pair, "y", ring(4, k))) for k in (1, 3, 2)]
    u_own, k_own, kt_own, edge = small(
        prep_body,
        [pair, *around, core_s],
        [((rank, cells), bf16, True), ((rank, cells), bf16, True), ((cells, rank), bf16, True), ((rank, cells // 2), bf16, True)],
        at=where_at,
    )
    u_oth = resident(lax.ppermute(u_own, "c", swap))
    chips = n_space // 2
    hops = [(2 * i + 1, 2 * i + 2) for i in range(chips - 1)] + [(2 * i + 2, 2 * i + 1) for i in range(chips - 1)]
    halo = resident(lax.ppermute(edge, SPACE, hops))

    growth = 0.5 + 0.5 * lax.dynamic_slice_in_dim(sample_class, core_at * half, half, 0).astype(f32)
    growth = resident(growth.reshape(1, half))
    scale = step_size * cell_weight
    quart = half // 2
    main = lambda start, kinds, back: functools.partial(part_body, start, kinds, back)
    l_first, ov_first = small(
        main(0, 0, False), [kt_own, u_own, v, growth], [((rank, quart), f32, True), ((cells, rank), f32, True)]
    )
    kt_oth, base, m_own = small(
        functools.partial(mid_body, rows_y, cols_z),
        [u_oth, core_s, k_own, halo, face_class, u_own],
        [((cells, rank), bf16, True), ((narrow, cells), f32, False), ((rank, rank), f32, True)],
        [((rank, cells), f32), ((rank, cells), bf16), ((7,) + face_class.shape[1:], f32), ((rank, cells), f32)],
        at=where_at,
        held=(ov_first, kt_own, l_first),
    )
    m_oth = resident(lax.ppermute(m_own, "c", swap))
    l_most, ov_send = small(
        main(0, 1, True),
        [kt_oth, u_oth, v, growth, l_first],
        [((rank, half), f32, True), ((rank, cells), bf16, True)],
        [((cells, rank), f32)],
        held=(ov_first, kt_own, u_own),
    )
    got = resident(lax.ppermute(ov_send, "c", swap))
    l_more, ov_more = small(
        main(quart, 2, False),
        [kt_own, u_own, v, growth, ov_first],
        [((rank, quart // 2), f32, True), ((cells, rank), f32, True)],
        held=(l_most, ov_send),
    )
    rows = rank // 4
    l_part, me, up, dn, away = small(
        functools.partial(last_body, scale),
        [kt_own, u_own, v, growth, l_most, l_more, ov_more, got, m_own, m_oth, core_s],
        [((rank, half), bf16, None), ((rows, cells), f32, True)] + [((rows, cells), bf16, True)] * 3,
        [
            ((cells, rank), f32),
            ((rank, cells), f32),
            ((2 * rank, rank), bf16),
            ((rank, half), bf16),
            pltpu.SemaphoreType.DMA((2,)),
        ],
        at=where_at,
    )

    l_got = lax.all_to_all(l_part, SPACE, 0, 0, tiled=True)
    (l_new,) = small(
        gain_body, [resident(l_got.reshape(n_space // 2, 2, lanes, half))], [((lanes, samp_rows), f32, False)]
    )

    near = []
    for part, k in ((up, 1), (dn, 3), (away, 2)):
        near.append(resident(lax.ppermute(part, "y", ring(4, k))))
    mine, send = small(
        pair_body,
        [me, *near],
        [((narrow, cells), f32, True), ((narrow, cells), bf16, True)],
        [((rows, cells), f32)],
        at=where_at,
    )
    last = resident(lax.ppermute(send, "xh", swap))
    (k_new,) = small(
        functools.partial(done_body, step_size * samp_weight),
        [base, mine, last],
        [(basis_u.shape, f32, False)],
    )
    return (k_new, l_new)


def solution(mesh):
    fine = Mesh(mesh.devices.reshape(4, 2, 2, 4, 2), SPACE + SAMP)
    return jax.shard_map(
        per_device,
        mesh=fine,
        in_specs=(P(SAMP, SPACE, None, None), P(SPACE, SAMP), P(), P(None, SPACE, None, None), P(SAMP)),
        out_specs=(P(SAMP, SPACE, None, None), P(SPACE, SAMP)),
        check_vma=False,
    )
```
